512 devices in a mesh: grid: 32 (over y, x, core), pts: 16 (over z).
Axes of the slice: x: 4, y: 4, z: 16, core: 2. Of those that a mesh axis runs over, the one named last changes fastest.
Arguments:
- orbitals: bfloat16 [512, 16384], P(None, 'grid'), may hold values from -0.8984375 to 0.8984375
- point_index: int32 [8192], P('pts'), may hold values from 0 to 16383
Outputs:
- screened: float32 [16, 512, 128, 128], P('pts', 'grid')
The draws below stay inside these ranges and needn't reach their ends.
All inputs are finite; a program needn't handle non-finite values.
Results may differ from the reference program's by a relative error of at most 0.0003.
Values may be sent and summed in bfloat16 or wider, within the bound.
A program may use at most 64 MiB of HBM per device.

```python
import jax
import jax.numpy as jnp
from jax import lax

SIDE = 128
NORB = 512
NPTS = 8192
NG = 16384
N_PTS = 16


def set_ends(array, key, low, top_value):
    dims = array.shape
    index_at = [jax.random.randint(jax.random.fold_in(key, axis), (), 0, dims[axis]) for axis in range(len(dims))]
    array = array.at[tuple(index_at)].set(low)
    longest = dims.index(max(dims))
    index_at[longest] = (index_at[longest] + 1) % dims[longest]
    return array.at[tuple(index_at)].set(top_value)


def levels(own_key, extent, shards, least, largest):
    def one(axis_at, shards_of):
        draws = jax.random.uniform(jax.random.fold_in(jax.random.fold_in(own_key, 6), axis_at), (shards_of,), jnp.float32, least / len(shards), largest / len(shards))
        return jnp.repeat(jnp.exp(draws), extent[axis_at] // shards_of).reshape((-1,) + (1,) * (len(extent) - axis_at - 1))

    gain = one(*shards[0])
    for cut in shards[1:]:
        gain = gain * one(*cut)
    return gain


def scatter_about(stream_key, shape, width, reach, pieces=(), held_as=jnp.bfloat16):
    entries = width * jax.random.normal(stream_key, shape, jnp.float32)
    if pieces:
        entries = entries * levels(stream_key, shape, pieces, -0.22, 0.18)
    return jnp.clip(entries, -reach, reach).astype(held_as)


def setup_inputs(seed: int = 0) -> dict:
    key_of = jax.random.split(jax.random.key(seed), 3)
    return {
        "orbitals": scatter_about(key_of[0], (NORB, NG), 0.15, 0.8984375, ((1, 32),)),
        "point_index": set_ends(jax.random.randint(key_of[1], (NPTS,), 0, NG), jax.random.fold_in(key_of[1], 1), 0, NG - 1).astype(jnp.int32),
    }


def screen_kernel():
    frequency = jnp.arange(SIDE, dtype=jnp.int32)
    wavenumber = jnp.minimum(frequency, SIDE - frequency).astype(jnp.float32)
    screening = SIDE / 16.0
    values = screening / jnp.sqrt(wavenumber[:, None] ** 2 + wavenumber[None, :] ** 2 + screening * screening)
    anchor = (frequency[:, None] == 0) & (frequency[None, :] == 0)
    return jnp.where(anchor, jnp.zeros_like(values), values)

def reference(orbitals, point_index):
    picked = jnp.take(orbitals, point_index, axis=1)
    kernel_values = screen_kernel()
    block_points = min(256, NPTS)
    chosen_blocks = picked.reshape(NORB, NPTS // block_points, block_points).transpose(1, 0, 2)

    def one_block(chosen_rows):
        pair_values = jnp.dot(chosen_rows.T, orbitals, preferred_element_type=jnp.float32)
        squared = (pair_values * pair_values).reshape(block_points, SIDE, SIDE)
        spectrum = jnp.fft.fft2(squared) * kernel_values
        return jnp.real(jnp.fft.ifft2(spectrum)).astype(jnp.float32)
    result = lax.map(one_block, chosen_blocks)
    return result.reshape(N_PTS, NPTS // N_PTS, SIDE, SIDE)
```

```python
import functools
import math

import jax
import jax.numpy as jnp
from jax import lax
from jax.experimental import pallas as pl
from jax.experimental.pallas import tpu as pltpu
from jax.sharding import PartitionSpec as P

SIDE = 128
MESH = pl.DeviceIdType.MESH
F32 = jnp.float32
BF16 = jnp.bfloat16
TOP = 32766.0
FLOOR = 1e-30


def split(values):
    high = values.astype(BF16)
    return high, (values - high.astype(F32)).astype(BF16)


def cas_table():
    rows = lax.broadcasted_iota(jnp.int32, (SIDE, SIDE), 0)
    columns = lax.broadcasted_iota(jnp.int32, (SIDE, SIDE), 1)
    angles = ((rows * columns) % SIDE).astype(F32) * (2.0 * math.pi / SIDE)
    return jnp.cos(angles) + jnp.sin(angles)


def screen_kernel():
    rows = lax.broadcasted_iota(jnp.int32, (SIDE, SIDE), 0)
    columns = lax.broadcasted_iota(jnp.int32, (SIDE, SIDE), 1)
    across = jnp.minimum(rows, SIDE - rows).astype(F32)
    along = jnp.minimum(columns, SIDE - columns).astype(F32)
    screening = SIDE / 16.0
    values = screening / jnp.sqrt(across * across + along * along + screening * screening)
    return jnp.where((rows == 0) & (columns == 0), 0.0, values * (1.0 / (SIDE * SIDE)))


def offsets(size_y, size_x):
    far = lambda d, n: min(d, n - d)
    every = [(dy, dx) for dy in range(size_y) for dx in range(size_x) if (dy, dx) != (0, 0)]
    return sorted(every, key=lambda o: (far(o[0], size_y) + far(o[1], size_x), o))


def body(
    size_y, size_x, points,
    orb_hbm, idx_hbm, out_ref,
    phi, idx, partial, got, vectors, quant, scale, quant_in, scale_in, rows_done, wide, tall, kern,
    load_sem, sib_send, sib_recv, rs_send, rs_recv, ag_send, ag_recv, q_send, q_recv, s_send, s_recv,
):
    me = lax.axis_index("grid")
    core = me % 2
    chip = me // 2
    my_y = chip // size_x
    my_x = chip % size_x
    chips = size_y * size_x
    cells = phi.shape[2]
    offs = offsets(size_y, size_x)

    def at(dy, dx):
        return ((my_y + dy + size_y) % size_y) * size_x + (my_x + dx + size_x) % size_x

    def device(c):
        return {"grid": c * 2 + core}

    sibling = {"grid": chip * 2 + 1 - core}

    barrier = pltpu.get_barrier_semaphore()
    pl.semaphore_signal(barrier, inc=1, device_id=sibling, device_id_type=MESH)
    for dy, dx in offs:
        pl.semaphore_signal(barrier, inc=1, device_id=device(at(dy, dx)), device_id_type=MESH)

    load_orb = pltpu.make_async_copy(orb_hbm, phi.at[core], load_sem.at[0])
    load_orb.start()
    load_idx = pltpu.make_async_copy(idx_hbm, idx, load_sem.at[1])
    load_idx.start()

    high, low = split(cas_table())
    wide[0:SIDE, 0:SIDE] = high
    wide[0:SIDE, SIDE:] = low
    wide[SIDE:, 0:SIDE] = high
    wide[SIDE:, SIDE:] = low
    tall[0:SIDE, 0:SIDE] = high
    tall[0:SIDE, SIDE:] = high
    tall[SIDE:, 0:SIDE] = low
    tall[SIDE:, SIDE:] = low
    kern[...] = screen_kernel()

    load_idx.wait()
    total = idx.shape[1]
    column = jnp.transpose(jnp.broadcast_to(idx[...], (SIDE, total)))
    column = column.reshape(chips, 2, points, SIDE)
    column = jnp.where(core == 0, column[:, 0], column[:, 1]).reshape(chips * points, SIDE)
    column = column - chip * (2 * cells)
    lane = lax.broadcasted_iota(jnp.int32, (chips * points, SIDE), 1)

    def owned(half):
        parts = [
            jnp.where(column == lane + (half * cells + j * SIDE), 1.0, 0.0).astype(BF16)
            for j in range(cells // SIDE)
        ]
        mask = jnp.concatenate(parts, axis=1)
        return lax.dot_general(mask, phi[half], (((1,), (1,)), ((), ())), preferred_element_type=F32)

    load_orb.wait()
    pl.semaphore_wait(barrier, len(offs) + 1)

    to_sibling = pltpu.make_async_remote_copy(
        src_ref=phi.at[core], dst_ref=phi.at[core], send_sem=sib_send, recv_sem=sib_recv,
        device_id=sibling, device_id_type=MESH,
    )
    to_sibling.start()
    to_sibling.wait()

    own = (owned(0) + owned(1)).astype(BF16)
    partial[...] = own.reshape(chips, points, own.shape[1])

    def rs_copy(d):
        dy, dx = offs[d]
        peer = at(dy, dx)
        return pltpu.make_async_remote_copy(
            src_ref=partial.at[peer], dst_ref=got.at[d], send_sem=rs_send.at[d], recv_sem=rs_recv.at[d],
            device_id=device(peer), device_id_type=MESH,
        )

    rs = [rs_copy(d) for d in range(len(offs))]
    for copy in reversed(rs):
        copy.start()
    mine = partial[chip].astype(F32)
    for d, copy in enumerate(rs):
        copy.wait_recv()
        mine = mine + got[d].astype(F32)
    vectors[0] = mine.astype(BF16)

    def ag_copy(d):
        dy, dx = offs[d]
        return pltpu.make_async_remote_copy(
            src_ref=vectors.at[0], dst_ref=vectors.at[d + 1], send_sem=ag_send.at[d], recv_sem=ag_recv.at[d],
            device_id=device(at(dy, dx)), device_id_type=MESH,
        )

    ag = [ag_copy(d) for d in range(len(offs))]
    for copy in reversed(ag):
        copy.start()

    def back_copies(d):
        dy, dx = offs[d]
        to = device(at(-dy, -dx))
        first = pltpu.make_async_remote_copy(
            src_ref=quant.at[d + 1], dst_ref=quant_in.at[d + 1], send_sem=q_send.at[d], recv_sem=q_recv.at[d],
            device_id=to, device_id_type=MESH,
        )
        second = pltpu.make_async_remote_copy(
            src_ref=scale.at[d + 1], dst_ref=scale_in.at[d + 1], send_sem=s_send.at[d], recv_sem=s_recv.at[d],
            device_id=to, device_id_type=MESH,
        )
        return first, second

    back = [back_copies(d) for d in range(len(offs))]
    diagonal = lax.broadcasted_iota(jnp.int32, (points, SIDE), 0) == lax.broadcasted_iota(
        jnp.int32, (points, SIDE), 1
    )

    group = 4
    for start in range(0, chips, group):
        for slot in range(start, start + group):
            if slot > 0:
                ag[slot - 1].wait_recv()
        block = vectors[start : start + group].reshape(group * points, vectors.shape[2])
        pair = jnp.concatenate(
            [jnp.dot(block, phi[h], preferred_element_type=F32) for h in range(2)], axis=1
        )
        peak = jnp.maximum(jnp.max(jnp.abs(pair), axis=1, keepdims=True), FLOOR)
        coded = jnp.round(pair * (TOP / peak)).astype(jnp.int32).astype(jnp.int16)
        quant[start : start + group] = coded.reshape(group, points, 2 * cells)
        step = jnp.broadcast_to(peak * (1.0 / TOP), (group * points, SIDE))
        for slot in range(start, start + group):
            piece = step[(slot - start) * points : (slot - start + 1) * points]
            scale[slot] = jnp.sum(jnp.where(diagonal, piece, 0.0), axis=0, keepdims=True)
        for slot in range(start, start + group):
            if slot > 0:
                for copy in back[slot - 1]:
                    copy.start()

    rows = 2 * cells // SIDE

    def along(block, row_of, source):
        step = jnp.sum(
            jnp.where(diagonal, jnp.broadcast_to(row_of, (points, SIDE)), 0.0), axis=1, keepdims=True
        )
        pair = block.astype(jnp.int32).astype(F32) * step
        square = pair * pair
        stacked = jnp.concatenate([square[:, r * SIDE : (r + 1) * SIDE] for r in range(rows)], axis=0)
        high, low = split(stacked)
        product = jnp.dot(jnp.concatenate([high, low], axis=1), wide[...], preferred_element_type=F32)
        at_row = pl.multiple_of(source * (rows * points), rows * points)
        rows_done[pl.ds(at_row, rows * points), :] = product[:, :SIDE] + product[:, SIDE:]

    along(quant[0], scale[0], chip)
    for d in range(len(offs)):
        for copy in back[d]:
            copy.wait_recv()
        dy, dx = offs[d]
        along(quant_in[d + 1], scale_in[d + 1], at(dy, dx))

    weight = jnp.concatenate([kern[...], kern[...]], axis=1)
    for first in range(0, points, 2):
        pieces = [rows_done[pl.ds(p, SIDE, stride=points), :] for p in (first, first + 1)]
        values = jnp.concatenate(pieces, axis=1)
        for turn in range(2):
            high, low = split(values)
            product = jnp.dot(tall[...], jnp.concatenate([high, low], axis=0), preferred_element_type=F32)
            values = product[:SIDE] + product[SIDE:]
            if turn == 0:
                values = values * weight
        high, low = split(values)
        for p in range(2):
            lanes = slice(p * SIDE, (p + 1) * SIDE)
            operand = jnp.concatenate([high[:, lanes], low[:, lanes]], axis=1)
            product = jnp.dot(operand, wide[...], preferred_element_type=F32)
            out_ref[first + p] = product[:, :SIDE] + product[:, SIDE:]

    for copy in rs:
        copy.wait_send()
    for copy in ag:
        copy.wait_send()
    for pair_of in back:
        for copy in pair_of:
            copy.wait_send()


def shards(size_y, size_x, orbitals, point_index):
    orbital_count, cells = orbitals.shape
    chips = size_y * size_x
    points = point_index.shape[0] // (2 * chips)
    others = chips - 1
    dma = pltpu.SemaphoreType.DMA
    out = pl.pallas_call(
        functools.partial(body, size_y, size_x, points),
        out_shape=jax.ShapeDtypeStruct((points, SIDE, SIDE), F32),
        in_specs=[pl.BlockSpec(memory_space=pl.ANY)] * 2,
        out_specs=pl.BlockSpec(memory_space=pltpu.VMEM),
        scratch_shapes=[
            pltpu.VMEM((2, orbital_count, cells), BF16),
            pltpu.VMEM((1, point_index.shape[0]), jnp.int32),
            pltpu.VMEM((chips, points, orbital_count), BF16),
            pltpu.VMEM((others, points, orbital_count), BF16),
            pltpu.VMEM((chips, points, orbital_count), BF16),
            pltpu.VMEM((chips, points, 2 * cells), jnp.int16),
            pltpu.VMEM((chips, 1, SIDE), F32),
            pltpu.VMEM((chips, points, 2 * cells), jnp.int16),
            pltpu.VMEM((chips, 1, SIDE), F32),
            pltpu.VMEM((SIDE * points, SIDE), F32),
            pltpu.VMEM((2 * SIDE, 2 * SIDE), BF16),
            pltpu.VMEM((2 * SIDE, 2 * SIDE), BF16),
            pltpu.VMEM((SIDE, SIDE), F32),
            dma((2,)), dma, dma,
            dma((others,)), dma((others,)), dma((others,)), dma((others,)),
            dma((others,)), dma((others,)), dma((others,)), dma((others,)),
        ],
        compiler_params=pltpu.CompilerParams(collective_id=0, has_side_effects=True),
    )(orbitals, point_index.reshape(1, -1))
    return out[None]


def solution(mesh):
    grid_count = mesh.shape["grid"]
    size = math.isqrt(grid_count // 2)
    in_specs = (P(None, "grid"), P("pts"))
    out_specs = P("pts", "grid", None, None)
    step = functools.partial(shards, size, size)
    return jax.shard_map(step, mesh=mesh, in_specs=in_specs, out_specs=out_specs, check_vma=False)
```

```python
import functools
import math

import jax
import jax.numpy as jnp
from jax import lax
from jax.experimental import pallas as pl
from jax.experimental.pallas import tpu as pltpu
from jax.sharding import PartitionSpec as P

SIDE = 128
MESH = pl.DeviceIdType.MESH
F32 = jnp.float32
BF16 = jnp.bfloat16
TOP = 32766.0
FLOOR = 1e-30
PARTS = 2
PAIR_GROUP = 8
ROW_GROUP = 4
VMEM_BYTES = 16 * 1024 * 1024


def split(values):
    high = values.astype(BF16)
    return high, (values - high.astype(F32)).astype(BF16)


def cas_table():
    rows = lax.broadcasted_iota(jnp.int32, (SIDE, SIDE), 0)
    columns = lax.broadcasted_iota(jnp.int32, (SIDE, SIDE), 1)
    angles = ((rows * columns) % SIDE).astype(F32) * (2.0 * math.pi / SIDE)
    return jnp.cos(angles) + jnp.sin(angles)


def screen_kernel():
    rows = lax.broadcasted_iota(jnp.int32, (SIDE, SIDE), 0)
    columns = lax.broadcasted_iota(jnp.int32, (SIDE, SIDE), 1)
    across = jnp.minimum(rows, SIDE - rows).astype(F32)
    along = jnp.minimum(columns, SIDE - columns).astype(F32)
    screening = SIDE / 16.0
    values = screening / jnp.sqrt(across * across + along * along + screening * screening)
    return jnp.where((rows == 0) & (columns == 0), 0.0, values * (1.0 / (SIDE * SIDE)))


def offsets(size_y, size_x):
    far = lambda d, n: min(d, n - d)
    every = [(dy, dx) for dy in range(size_y) for dx in range(size_x) if (dy, dx) != (0, 0)]
    return sorted(every, key=lambda o: (-far(o[0], size_y) - far(o[1], size_x), o))


def body(
    size_y, size_x, points,
    orb_hbm, idx_hbm, out_ref,
    phi, idx, first_sum, partial, got, vectors, quant, scale, quant_in, scale_in, rows_done, wide, tall, kern, middle,
    last,
    load_sem, sib_send, sib_recv, rs_send, rs_recv, ag_send, ag_recv, q_send, q_recv, s_send, s_recv,
):
    me = lax.axis_index("grid")
    core = me % 2
    chip = me // 2
    my_y = chip // size_x
    my_x = chip % size_x
    chips = size_y * size_x
    cells = phi.shape[2]
    offs = offsets(size_y, size_x)
    count = len(offs)
    others = range(count)
    depth = phi.shape[1] // PARTS
    parts = range(PARTS)

    def at(dy, dx):
        return ((my_y + dy + size_y) % size_y) * size_x + (my_x + dx + size_x) % size_x

    def device(c):
        return {"grid": c * 2 + core}

    def remote(src, dst, send, recv, to):
        return pltpu.make_async_remote_copy(
            src_ref=src, dst_ref=dst, send_sem=send, recv_sem=recv, device_id=to, device_id_type=MESH
        )

    def wait_all(ref, sem):
        pltpu.make_async_copy(ref, ref, sem).wait()

    sibling = {"grid": chip * 2 + 1 - core}

    with jax.named_scope("signals"):
        load_orb = pltpu.make_async_copy(orb_hbm, phi.at[core], load_sem.at[0])
        load_orb.start()
        load_idx = pltpu.make_async_copy(idx_hbm, idx, load_sem.at[1])
        load_idx.start()
        barrier = pltpu.get_barrier_semaphore()
        pl.semaphore_signal(barrier, inc=1, device_id=sibling, device_id_type=MESH)
        for dy, dx in offs:
            pl.semaphore_signal(barrier, inc=1, device_id=device(at(dy, dx)), device_id_type=MESH)

    with jax.named_scope("barrier"):
        pl.semaphore_wait(barrier, count + 1)

    def band(p):
        return pl.ds(p * depth, depth)

    to_sibling = [
        remote(orb_hbm.at[band(p)], phi.at[core, band(p)], sib_send.at[p], sib_recv.at[p], sibling) for p in parts
    ]
    for copy in to_sibling:
        copy.start()

    with jax.named_scope("indices"):
        load_idx.wait()
        total = idx.shape[1]
        column = jnp.transpose(jnp.broadcast_to(idx[...], (SIDE, total)))
        column = column.reshape(chips, 2, points, SIDE)
        column = jnp.where(core == 0, column[:, 0], column[:, 1]).reshape(chips * points, SIDE)
        column = column - chip * (2 * cells)
        lane = lax.broadcasted_iota(jnp.int32, (chips * points, SIDE), 1)

    def mask_of(half):
        return jnp.concatenate(
            [
                jnp.where(column == lane + (half * cells + j * SIDE), 1.0, 0.0).astype(BF16)
                for j in range(cells // SIDE)
            ],
            axis=1,
        )

    def owned(mask, values):
        return lax.dot_general(mask, values, (((1,), (1,)), ((), ())), preferred_element_type=F32)

    with jax.named_scope("ownpicks"):
        load_orb.wait()
        first_sum[...] = owned(mask_of(core), phi[core])
        theirs = mask_of(1 - core)

    def rs_copy(p, d):
        peer = at(*offs[d])
        return remote(partial.at[p, peer], got.at[p, d], rs_send, rs_recv.at[p], device(peer))

    for p in parts:
        with jax.named_scope("sibling%d" % p):
            to_sibling[p].wait()
        with jax.named_scope("picks%d" % p):
            lanes = slice(p * depth, (p + 1) * depth)
            own = first_sum[:, lanes] + owned(theirs, phi[1 - core, lanes])
            partial[p] = own.astype(BF16).reshape(chips, points, depth)
            for d in others:
                rs_copy(p, d).start()

    with jax.named_scope("tables"):
        high, low = split(cas_table())
        wide[0:SIDE, 0:SIDE] = high
        wide[0:SIDE, SIDE:] = low
        wide[SIDE:, 0:SIDE] = high
        wide[SIDE:, SIDE:] = low
        tall[0:SIDE, 0:SIDE] = high
        tall[0:SIDE, SIDE:] = high
        tall[SIDE:, 0:SIDE] = low
        tall[SIDE:, SIDE:] = low
        kern[...] = screen_kernel()

    starts = range(0, chips, PAIR_GROUP)

    def ag_copy(p, d):
        return remote(
            vectors.at[p, count], vectors.at[p, d], ag_send, ag_recv.at[p, d // PAIR_GROUP], device(at(*offs[d]))
        )

    for p in parts:
        with jax.named_scope("scatter%d" % p):
            wait_all(got.at[p], rs_recv.at[p])
            mine = partial[p, chip].astype(F32)
            for d in others:
                mine = mine + got[p, d].astype(F32)
            vectors[p, count] = mine.astype(BF16)
            for d in others:
                ag_copy(p, d).start()

    def back_copies(d):
        dy, dx = offs[d]
        to = device(at(-dy, -dx))
        g = d // ROW_GROUP
        first = remote(quant.at[d], quant_in.at[d], q_send, q_recv.at[g], to)
        second = remote(scale.at[d], scale_in.at[d], s_send, s_recv.at[g], to)
        return first, second

    diagonal = lax.broadcasted_iota(jnp.int32, (points, SIDE), 0) == lax.broadcasted_iota(
        jnp.int32, (points, SIDE), 1
    )

    for g, start in enumerate(starts):
        size = min(PAIR_GROUP, chips - start)
        group = range(start, start + size)
        with jax.named_scope("gather%d" % start):
            for p in parts:
                here = pl.ds(start, min(size, count - start))
                wait_all(vectors.at[p, here], ag_recv.at[p, g])
        with jax.named_scope("pairs%d" % start):
            halves = []
            for h in range(2):
                pair = None
                for p in parts:
                    block = vectors[p, start : start + size].reshape(size * points, depth)
                    term = jnp.dot(block, phi[h, band(p)], preferred_element_type=F32)
                    pair = term if pair is None else pair + term
                halves.append(pair)
            pair = jnp.concatenate(halves, axis=1)
            peak = jnp.maximum(jnp.max(jnp.abs(pair), axis=1, keepdims=True), FLOOR)
            coded = jnp.round(pair * (TOP / peak)).astype(jnp.int32).astype(jnp.int16)
            quant[start : start + size] = coded.reshape(size, points, 2 * cells)
            step = jnp.broadcast_to(peak * (1.0 / TOP), (size * points, SIDE))
            for slot in group:
                piece = step[(slot - start) * points : (slot - start + 1) * points]
                scale[slot] = jnp.sum(jnp.where(diagonal, piece, 0.0), axis=0, keepdims=True)
            for slot in group:
                if slot < count:
                    for copy in back_copies(slot):
                        copy.start()

    rows = 2 * cells // SIDE

    def along(blocks):
        stacks = []
        for block, row_of, _ in blocks:
            step = jnp.sum(
                jnp.where(diagonal, jnp.broadcast_to(row_of, (points, SIDE)), 0.0), axis=1, keepdims=True
            )
            pair = block.astype(jnp.int32).astype(F32) * step
            square = pair * pair
            stacks.extend(square[:, r * SIDE : (r + 1) * SIDE] for r in range(rows))
        high, low = split(jnp.concatenate(stacks, axis=0))
        product = jnp.dot(jnp.concatenate([high, low], axis=1), wide[...], preferred_element_type=F32)
        product = product[:, :SIDE] + product[:, SIDE:]
        size = rows * points
        for n, (_, _, source) in enumerate(blocks):
            rows_done[pl.ds(pl.multiple_of(source * size, size), size), :] = product[n * size : (n + 1) * size]

    for g, start in enumerate(range(0, chips, ROW_GROUP)):
        size = min(ROW_GROUP, chips - start)
        with jax.named_scope("wait%d" % start):
            here = pl.ds(start, min(size, count - start))
            wait_all(quant_in.at[here], q_recv.at[g])
            wait_all(scale_in.at[here], s_recv.at[g])
        with jax.named_scope("along%d" % start):
            along([
                (quant_in[s], scale_in[s], at(*offs[s])) if s < count else (quant[s], scale[s], chip)
                for s in range(start, start + size)
            ])

    with jax.named_scope("across"):
        weight = jnp.concatenate([kern[...], kern[...]], axis=1)
        for first in range(0, points, 2):
            pieces = [rows_done[pl.ds(p, SIDE, stride=points), :] for p in (first, first + 1)]
            high, low = split(jnp.concatenate(pieces, axis=1))
            product = jnp.dot(tall[...], jnp.concatenate([high, low], axis=0), preferred_element_type=F32)
            high, low = split((product[:SIDE] + product[SIDE:]) * weight)
            middle[first // 2, 0:SIDE] = high
            middle[first // 2, SIDE:] = low
    with jax.named_scope("inverse"):
        for first in range(0, points, 2):
            product = jnp.dot(tall[...], middle[first // 2], preferred_element_type=F32)
            high, low = split(product[:SIDE] + product[SIDE:])
            for p in range(2):
                lanes = slice(p * SIDE, (p + 1) * SIDE)
                last[first + p, :, 0:SIDE] = high[:, lanes]
                last[first + p, :, SIDE:] = low[:, lanes]
    with jax.named_scope("output"):
        for first in range(0, points, 2):
            product = jnp.dot(
                last[first : first + 2].reshape(2 * SIDE, 2 * SIDE), wide[...], preferred_element_type=F32
            )
            out_ref[first : first + 2] = (product[:, :SIDE] + product[:, SIDE:]).reshape(2, SIDE, SIDE)

    with jax.named_scope("sends"):
        wait_all(got, rs_send)
        wait_all(vectors.at[:, pl.ds(0, count)], ag_send)
        wait_all(quant_in, q_send)
        wait_all(scale_in, s_send)


def shards(size_y, size_x, orbitals, point_index):
    orbital_count, cells = orbitals.shape
    chips = size_y * size_x
    points = point_index.shape[0] // (2 * chips)
    others = chips - 1
    depth = orbital_count // PARTS
    dma = pltpu.SemaphoreType.DMA
    in_place = functools.partial(pltpu.with_memory_space_constraint, memory_space=pltpu.HBM)
    out = pl.pallas_call(
        functools.partial(body, size_y, size_x, points),
        out_shape=jax.ShapeDtypeStruct((points, SIDE, SIDE), F32),
        in_specs=[pl.BlockSpec(memory_space=pltpu.HBM)] * 2,
        out_specs=pl.BlockSpec(memory_space=pltpu.VMEM),
        scratch_shapes=[
            pltpu.VMEM((2, orbital_count, cells), BF16),
            pltpu.VMEM((1, point_index.shape[0]), jnp.int32),
            pltpu.VMEM((chips * points, orbital_count), F32),
            pltpu.VMEM((PARTS, chips, points, depth), BF16),
            pltpu.VMEM((PARTS, others, points, depth), BF16),
            pltpu.VMEM((PARTS, chips, points, depth), BF16),
            pltpu.VMEM((chips, points, 2 * cells), jnp.int16),
            pltpu.VMEM((chips, 1, SIDE), F32),
            pltpu.VMEM((others, points, 2 * cells), jnp.int16),
            pltpu.VMEM((others, 1, SIDE), F32),
            pltpu.VMEM((SIDE * points, SIDE), F32),
            pltpu.VMEM((2 * SIDE, 2 * SIDE), BF16),
            pltpu.VMEM((2 * SIDE, 2 * SIDE), BF16),
            pltpu.VMEM((SIDE, SIDE), F32),
            pltpu.VMEM((points // 2, 2 * SIDE, 2 * SIDE), BF16),
            pltpu.VMEM((points, SIDE, 2 * SIDE), BF16),
            dma((2,)), dma((PARTS,)), dma((PARTS,)),
            dma, dma((PARTS,)), dma, dma((PARTS, pl.cdiv(chips, PAIR_GROUP))),
            dma, dma((pl.cdiv(chips, ROW_GROUP),)), dma, dma((pl.cdiv(chips, ROW_GROUP),)),
        ],
        compiler_params=pltpu.CompilerParams(
            collective_id=0, has_side_effects=True, vmem_limit_bytes=VMEM_BYTES
        ),
    )(in_place(orbitals), in_place(point_index.reshape(1, -1)))
    return out[None]


def solution(mesh):
    grid_count = mesh.shape["grid"]
    size = math.isqrt(grid_count // 2)
    in_specs = (P(None, "grid"), P("pts"))
    out_specs = P("pts", "grid", None, None)
    step = functools.partial(shards, size, size)
    return jax.shard_map(step, mesh=mesh, in_specs=in_specs, out_specs=out_specs, check_vma=False)
```

```python
import functools
import math

import jax
import jax.numpy as jnp
from jax import lax
from jax.experimental import pallas as pl
from jax.experimental.pallas import tpu as pltpu
from jax.sharding import PartitionSpec as P

SIDE = 128
MESH = pl.DeviceIdType.MESH
F32 = jnp.float32
BF16 = jnp.bfloat16
TOP = 32766.0
FLOOR = 1e-30
COLUMN_GROUPS = ((2, 1), (3, 0))
ROW_GROUP = 4
VMEM_BYTES = 16 * 1024 * 1024


def split(values):
    high = values.astype(BF16)
    return high, (values - high.astype(F32)).astype(BF16)


def cas_table():
    rows = lax.broadcasted_iota(jnp.int32, (SIDE, SIDE), 0)
    columns = lax.broadcasted_iota(jnp.int32, (SIDE, SIDE), 1)
    angles = ((rows * columns) % SIDE).astype(F32) * (2.0 * math.pi / SIDE)
    return jnp.cos(angles) + jnp.sin(angles)


def screen_kernel():
    rows = lax.broadcasted_iota(jnp.int32, (SIDE, SIDE), 0)
    columns = lax.broadcasted_iota(jnp.int32, (SIDE, SIDE), 1)
    across = jnp.minimum(rows, SIDE - rows).astype(F32)
    along = jnp.minimum(columns, SIDE - columns).astype(F32)
    screening = SIDE / 16.0
    values = screening / jnp.sqrt(across * across + along * along + screening * screening)
    return jnp.where((rows == 0) & (columns == 0), 0.0, values * (1.0 / (SIDE * SIDE)))


def offsets(size_y, size_x):
    far = lambda d, n: min(d, n - d)
    every = [(dy, dx) for dy in range(size_y) for dx in range(size_x) if (dy, dx) != (0, 0)]
    return sorted(every, key=lambda o: (-far(o[0], size_y) - far(o[1], size_x), o))


def body(
    side, points,
    orb_hbm, idx_hbm, out_ref,
    phi, idx, mine, theirs, from_sib, part, first_in, summed, second_in, vectors, quant, scale, quant_in, scale_in,
    rows_done, wide, tall, kern, middle, last,
    load_sem, sib_send, sib_recv, orb_send, orb_recv, p_send, first_recv, second_recv, third_recv,
    q_send, q_recv, s_send, s_recv,
):
    me = lax.axis_index("grid")
    core = me % 2
    chip = me // 2
    my_y = chip // side
    my_x = chip % side
    chips = side * side
    cells = phi.shape[2]
    orbital_count = phi.shape[1]
    half = orbital_count // 2
    offs = offsets(side, side)
    count = len(offs)
    steps = [2, 1, 3][-(side - 1) :]
    flavours = range(2)
    first_at = (my_x, my_y)

    def at(dy, dx):
        return ((my_y + dy + side) % side) * side + (my_x + dx + side) % side

    def device(c):
        return {"grid": c * 2 + core}

    def along_first(f, e):
        return device(at(0, e) if f == 0 else at(e, 0))

    def along_second(f, e):
        return device(at(e, 0) if f == 0 else at(0, e))

    def remote(src, dst, send, recv, to):
        return pltpu.make_async_remote_copy(
            src_ref=src, dst_ref=dst, send_sem=send, recv_sem=recv, device_id=to, device_id_type=MESH
        )

    def wait_all(ref, sem):
        pltpu.make_async_copy(ref, ref, sem).wait()

    sibling = {"grid": chip * 2 + 1 - core}

    with jax.named_scope("signals"):
        load_idx = pltpu.make_async_copy(idx_hbm, idx, load_sem.at[1])
        load_idx.start()
        load_orb = pltpu.make_async_copy(orb_hbm, phi.at[core], load_sem.at[0])
        load_orb.start()
        barrier = pltpu.get_barrier_semaphore()
        pl.semaphore_signal(barrier, inc=1, device_id=sibling, device_id_type=MESH)
        for e in steps:
            for f in flavours:
                pl.semaphore_signal(barrier, inc=1, device_id=along_first(f, e), device_id_type=MESH)

    with jax.named_scope("indices"):
        load_idx.wait()
        total = idx.shape[1]
        column = jnp.transpose(jnp.broadcast_to(idx[...], (SIDE, total))) - me * cells
        column = column.reshape(chips, 2, points, SIDE)
        lane = lax.broadcasted_iota(jnp.int32, (chips * points, SIDE), 1)

    def owned(layer, to):
        chosen = jnp.where(layer == 0, column[:, 0], column[:, 1]).reshape(chips * points, SIDE)
        mask = jnp.concatenate(
            [jnp.where(chosen == lane + j * SIDE, 1.0, 0.0).astype(BF16) for j in range(cells // SIDE)], axis=1
        )
        found = lax.dot_general(mask, phi[core], (((1,), (1,)), ((), ())), preferred_element_type=F32)
        found = found.astype(BF16)
        for y in range(side):
            for x in range(side):
                rows = slice((y * side + x) * points, (y * side + x + 1) * points)
                to[0, x, y] = found[rows, :half]
                to[1, y, x] = found[rows, half:]

    with jax.named_scope("ownpicks"):
        load_orb.wait()
        owned(1 - core, theirs)

    with jax.named_scope("barrier"):
        pl.semaphore_wait(barrier, 2 * len(steps) + 1)

    with jax.named_scope("sibstart"):
        for n, e in enumerate(steps + [0]):
            for f in flavours:
                line = (first_at[f] + e) % side
                remote(theirs.at[f, line], from_sib.at[n, f], sib_send, sib_recv.at[n], sibling).start()
        to_sibling = remote(phi.at[core], phi.at[core], orb_send, orb_recv, sibling)
        to_sibling.start()
    with jax.named_scope("minepicks"):
        owned(core, mine)

    for n, e in enumerate(steps + [0]):
        with jax.named_scope("sibling%d" % n):
            wait_all(from_sib.at[n], sib_recv.at[n])
        with jax.named_scope("first%d" % n):
            for f in flavours:
                line = (first_at[f] + e) % side
                part[n, f] = mine[f, line] + from_sib[n, f]
                if e:
                    remote(
                        part.at[n, f], first_in.at[f, n], p_send.at[0], first_recv.at[f], along_first(f, e)
                    ).start()

    with jax.named_scope("tables"):
        high, low = split(cas_table())
        wide[0:SIDE, 0:SIDE] = high
        wide[0:SIDE, SIDE:] = low
        wide[SIDE:, 0:SIDE] = high
        wide[SIDE:, SIDE:] = low
        tall[0:SIDE, 0:SIDE] = high
        tall[0:SIDE, SIDE:] = high
        tall[SIDE:, 0:SIDE] = low
        tall[SIDE:, SIDE:] = low
        kern[...] = screen_kernel()

    own_line = len(steps)
    for f in flavours:
        with jax.named_scope("firstwait%d" % f):
            wait_all(first_in.at[f], first_recv.at[f])
        with jax.named_scope("second%d" % f):
            value = part[own_line, f]
            for n in range(len(steps)):
                value = value + first_in[f, n]
            summed[f] = value
            for n, e in enumerate(steps):
                remote(
                    summed.at[f], second_in.at[f, n], p_send.at[1], second_recv.at[f], along_second(f, e)
                ).start()
    for f in flavours:
        with jax.named_scope("secondwait%d" % f):
            wait_all(second_in.at[f], second_recv.at[f])
        with jax.named_scope("third%d" % f):
            value = summed[f]
            for n in range(len(steps)):
                value = value + second_in[f, n]
            line = first_at[f]
            vectors[f, line] = value
            for e in steps:
                remote(
                    vectors.at[f, line], vectors.at[f, line], p_send.at[2], third_recv.at[f], along_first(f, e)
                ).start()

    def back_copies(d):
        dy, dx = offs[d]
        to = device(at(dy, dx))
        here = dx * side + (my_y + dy) % side
        g = d // ROW_GROUP
        first = remote(quant.at[here], quant_in.at[d], q_send, q_recv.at[g], to)
        second = remote(scale.at[here], scale_in.at[d], s_send, s_recv.at[g], to)
        return first, second

    diagonal = lax.broadcasted_iota(jnp.int32, (points, SIDE), 0) == lax.broadcasted_iota(
        jnp.int32, (points, SIDE), 1
    )

    with jax.named_scope("gather"):
        to_sibling.wait()
        for f in flavours:
            wait_all(first_in.at[f], third_recv.at[f])

    for group in COLUMN_GROUPS:
        with jax.named_scope("pairs%d" % group[0]):
            size = len(group) * side
            lines = [(my_x + r) % side for r in group]
            low_half = jnp.concatenate([vectors[0, c].reshape(side * points, half) for c in lines], axis=0)
            high_half = jnp.concatenate([vectors[1, y, c] for c in lines for y in range(side)], axis=0)
            block = jnp.concatenate([low_half, high_half], axis=1)
            pair = jnp.concatenate(
                [jnp.dot(block, phi[h], preferred_element_type=F32) for h in range(2)], axis=1
            )
            peak = jnp.maximum(jnp.max(jnp.abs(pair), axis=1, keepdims=True), FLOOR)
            coded = jnp.round(pair * (TOP / peak)).astype(jnp.int32).astype(jnp.int16)
            step = jnp.broadcast_to(peak * (1.0 / TOP), (size * points, SIDE))
            for n, r in enumerate(group):
                for y in range(side):
                    rows = slice((n * side + y) * points, (n * side + y + 1) * points)
                    quant[r * side + y] = coded[rows]
                    scale[r * side + y] = jnp.sum(jnp.where(diagonal, step[rows], 0.0), axis=0, keepdims=True)
            for d in range(count):
                if offs[d][1] in group:
                    for copy in back_copies(d):
                        copy.start()

    rows = 2 * cells // SIDE

    def along(blocks):
        stacks = []
        for block, row_of, _ in blocks:
            step = jnp.sum(
                jnp.where(diagonal, jnp.broadcast_to(row_of, (points, SIDE)), 0.0), axis=1, keepdims=True
            )
            pair = block.astype(jnp.int32).astype(F32) * step
            square = pair * pair
            stacks.extend(square[:, r * SIDE : (r + 1) * SIDE] for r in range(rows))
        high, low = split(jnp.concatenate(stacks, axis=0))
        product = jnp.dot(jnp.concatenate([high, low], axis=1), wide[...], preferred_element_type=F32)
        product = product[:, :SIDE] + product[:, SIDE:]
        size = rows * points
        for n, (_, _, source) in enumerate(blocks):
            rows_done[pl.ds(pl.multiple_of(source * size, size), size), :] = product[n * size : (n + 1) * size]

    for g, start in enumerate(range(0, chips, ROW_GROUP)):
        size = min(ROW_GROUP, chips - start)
        with jax.named_scope("wait%d" % start):
            here = pl.ds(start, min(size, count - start))
            wait_all(quant_in.at[here], q_recv.at[g])
            wait_all(scale_in.at[here], s_recv.at[g])
        with jax.named_scope("along%d" % start):
            along([
                (quant_in[s], scale_in[s], at(-offs[s][0], -offs[s][1]))
                if s < count
                else (quant[my_y], scale[my_y], chip)
                for s in range(start, start + size)
            ])

    with jax.named_scope("across"):
        weight = jnp.concatenate([kern[...], kern[...]], axis=1)
        for first in range(0, points, 2):
            pieces = [rows_done[pl.ds(p, SIDE, stride=points), :] for p in (first, first + 1)]
            high, low = split(jnp.concatenate(pieces, axis=1))
            product = jnp.dot(tall[...], jnp.concatenate([high, low], axis=0), preferred_element_type=F32)
            high, low = split((product[:SIDE] + product[SIDE:]) * weight)
            middle[first // 2, 0:SIDE] = high
            middle[first // 2, SIDE:] = low
    with jax.named_scope("inverse"):
        for first in range(0, points, 2):
            product = jnp.dot(tall[...], middle[first // 2], preferred_element_type=F32)
            high, low = split(product[:SIDE] + product[SIDE:])
            for p in range(2):
                lanes = slice(p * SIDE, (p + 1) * SIDE)
                last[first + p, :, 0:SIDE] = high[:, lanes]
                last[first + p, :, SIDE:] = low[:, lanes]
    with jax.named_scope("output"):
        for first in range(0, points, 2):
            product = jnp.dot(
                last[first : first + 2].reshape(2 * SIDE, 2 * SIDE), wide[...], preferred_element_type=F32
            )
            out_ref[first : first + 2] = (product[:, :SIDE] + product[:, SIDE:]).reshape(2, SIDE, SIDE)

    with jax.named_scope("sends"):
        wait_all(from_sib, sib_send)
        for n in range(3):
            wait_all(first_in, p_send.at[n])
        wait_all(quant_in, q_send)
        wait_all(scale_in, s_send)


def shards(side, orbitals, point_index):
    orbital_count, cells = orbitals.shape
    chips = side * side
    points = point_index.shape[0] // (2 * chips)
    others = chips - 1
    half = orbital_count // 2
    dma = pltpu.SemaphoreType.DMA
    in_place = functools.partial(pltpu.with_memory_space_constraint, memory_space=pltpu.HBM)
    row_groups = pl.cdiv(chips, ROW_GROUP)
    out = pl.pallas_call(
        functools.partial(body, side, points),
        out_shape=jax.ShapeDtypeStruct((points, SIDE, SIDE), F32),
        in_specs=[pl.BlockSpec(memory_space=pltpu.HBM)] * 2,
        out_specs=pl.BlockSpec(memory_space=pltpu.VMEM),
        scratch_shapes=[
            pltpu.VMEM((2, orbital_count, cells), BF16),
            pltpu.VMEM((1, point_index.shape[0]), jnp.int32),
            pltpu.VMEM((2, side, side, points, half), BF16),
            pltpu.VMEM((2, side, side, points, half), BF16),
            pltpu.VMEM((side, 2, side, points, half), BF16),
            pltpu.VMEM((side, 2, side, points, half), BF16),
            pltpu.VMEM((2, side - 1, side, points, half), BF16),
            pltpu.VMEM((2, side, points, half), BF16),
            pltpu.VMEM((2, side - 1, side, points, half), BF16),
            pltpu.VMEM((2, side, side, points, half), BF16),
            pltpu.VMEM((chips, points, 2 * cells), jnp.int16),
            pltpu.VMEM((chips, 1, SIDE), F32),
            pltpu.VMEM((others, points, 2 * cells), jnp.int16),
            pltpu.VMEM((others, 1, SIDE), F32),
            pltpu.VMEM((SIDE * points, SIDE), F32),
            pltpu.VMEM((2 * SIDE, 2 * SIDE), BF16),
            pltpu.VMEM((2 * SIDE, 2 * SIDE), BF16),
            pltpu.VMEM((SIDE, SIDE), F32),
            pltpu.VMEM((points // 2, 2 * SIDE, 2 * SIDE), BF16),
            pltpu.VMEM((points, SIDE, 2 * SIDE), BF16),
            dma((2,)), dma, dma((side,)), dma, dma,
            dma((3,)), dma((2,)), dma((2,)), dma((2,)),
            dma, dma((row_groups,)), dma, dma((row_groups,)),
        ],
        compiler_params=pltpu.CompilerParams(
            collective_id=0, has_side_effects=True, vmem_limit_bytes=VMEM_BYTES
        ),
    )(in_place(orbitals), in_place(point_index.reshape(1, -1)))
    return out[None]


def solution(mesh):
    grid_count = mesh.shape["grid"]
    size = math.isqrt(grid_count // 2)
    in_specs = (P(None, "grid"), P("pts"))
    out_specs = P("pts", "grid", None, None)
    step = functools.partial(shards, size)
    return jax.shard_map(step, mesh=mesh, in_specs=in_specs, out_specs=out_specs, check_vma=False)
```

```python
import functools
import math

import jax
import jax.numpy as jnp
from jax import lax
from jax.experimental import pallas as pl
from jax.experimental.pallas import tpu as pltpu
from jax.sharding import PartitionSpec as P

SIDE = 128
MESH = pl.DeviceIdType.MESH
F32 = jnp.float32
BF16 = jnp.bfloat16
TOP = 32766.0
FLOOR = 1e-30
COLUMN_GROUPS = ((2, 1, 3, 0),)
ROW_GROUP = 8
VMEM_BYTES = 16 * 1024 * 1024


def split(values):
    high = values.astype(BF16)
    return high, (values - high.astype(F32)).astype(BF16)


def cas_table():
    rows = lax.broadcasted_iota(jnp.int32, (SIDE, SIDE), 0)
    columns = lax.broadcasted_iota(jnp.int32, (SIDE, SIDE), 1)
    angles = ((rows * columns) % SIDE).astype(F32) * (2.0 * math.pi / SIDE)
    return jnp.cos(angles) + jnp.sin(angles)


def screen_kernel():
    rows = lax.broadcasted_iota(jnp.int32, (SIDE, SIDE), 0)
    columns = lax.broadcasted_iota(jnp.int32, (SIDE, SIDE), 1)
    across = jnp.minimum(rows, SIDE - rows).astype(F32)
    along = jnp.minimum(columns, SIDE - columns).astype(F32)
    screening = SIDE / 16.0
    values = screening / jnp.sqrt(across * across + along * along + screening * screening)
    return jnp.where((rows == 0) & (columns == 0), 0.0, values * (1.0 / (SIDE * SIDE)))


def offsets(size_y, size_x):
    far = lambda d, n: min(d, n - d)
    every = [(dy, dx) for dy in range(size_y) for dx in range(size_x) if (dy, dx) != (0, 0)]
    return sorted(every, key=lambda o: (-far(o[0], size_y) - far(o[1], size_x), o))


def body(
    side, points,
    orb_hbm, idx_hbm, last, wide,
    phi, idx, mine, theirs, from_sib, part, first_in, summed, second_in, vectors, quant, scale, quant_in, scale_in,
    rows_done, tall, kern, middle,
    load_sem, sib_send, sib_recv, orb_send, orb_recv, p_send, first_recv, second_recv, third_recv,
    q_send, q_recv, s_send, s_recv,
):
    me = lax.axis_index("grid")
    core = me % 2
    chip = me // 2
    my_y = chip // side
    my_x = chip % side
    chips = side * side
    cells = phi.shape[2]
    orbital_count = phi.shape[1]
    half = orbital_count // 2
    offs = offsets(side, side)
    count = len(offs)
    steps = [2, 1, 3][-(side - 1) :]
    flavours = range(2)
    first_at = (my_x, my_y)

    def at(dy, dx):
        return ((my_y + dy + side) % side) * side + (my_x + dx + side) % side

    def device(c):
        return {"grid": c * 2 + core}

    def along_first(f, e):
        return device(at(0, e) if f == 0 else at(e, 0))

    def along_second(f, e):
        return device(at(e, 0) if f == 0 else at(0, e))

    def remote(src, dst, send, recv, to):
        return pltpu.make_async_remote_copy(
            src_ref=src, dst_ref=dst, send_sem=send, recv_sem=recv, device_id=to, device_id_type=MESH
        )

    def wait_all(ref, sem):
        pltpu.make_async_copy(ref, ref, sem).wait()

    sibling = {"grid": chip * 2 + 1 - core}

    with jax.named_scope("signals"):
        load_idx = pltpu.make_async_copy(idx_hbm, idx, load_sem.at[1])
        load_idx.start()
        load_orb = pltpu.make_async_copy(orb_hbm, phi.at[core], load_sem.at[0])
        load_orb.start()
        barrier = pltpu.get_barrier_semaphore()
        pl.semaphore_signal(barrier, inc=1, device_id=sibling, device_id_type=MESH)
        for e in steps:
            for f in flavours:
                pl.semaphore_signal(barrier, inc=1, device_id=along_first(f, e), device_id_type=MESH)

    with jax.named_scope("indices"):
        load_idx.wait()
        total = idx.shape[1]
        column = jnp.transpose(jnp.broadcast_to(idx[...], (SIDE, total))) - me * cells
        column = column.reshape(chips, 2, points, SIDE)
        lane = lax.broadcasted_iota(jnp.int32, (chips * points, SIDE), 1)

    def owned(layer, to):
        chosen = jnp.where(layer == 0, column[:, 0], column[:, 1]).reshape(chips * points, SIDE)
        mask = jnp.concatenate(
            [jnp.where(chosen == lane + j * SIDE, 1.0, 0.0).astype(BF16) for j in range(cells // SIDE)], axis=1
        )
        found = lax.dot_general(mask, phi[core], (((1,), (1,)), ((), ())), preferred_element_type=F32)
        found = found.astype(BF16)
        for y in range(side):
            for x in range(side):
                rows = slice((y * side + x) * points, (y * side + x + 1) * points)
                to[0, x, y] = found[rows, :half]
                to[1, y, x] = found[rows, half:]

    with jax.named_scope("ownpicks"):
        load_orb.wait()
        owned(1 - core, theirs)

    with jax.named_scope("barrier"):
        pl.semaphore_wait(barrier, 2 * len(steps) + 1)

    with jax.named_scope("sibstart"):
        for n, e in enumerate(steps + [0]):
            for f in flavours:
                line = (first_at[f] + e) % side
                remote(theirs.at[f, line], from_sib.at[n, f], sib_send, sib_recv.at[n], sibling).start()
        to_sibling = remote(phi.at[core], phi.at[core], orb_send, orb_recv, sibling)
        to_sibling.start()
    with jax.named_scope("minepicks"):
        owned(core, mine)

    for n, e in enumerate(steps + [0]):
        with jax.named_scope("sibling%d" % n):
            wait_all(from_sib.at[n], sib_recv.at[n])
        with jax.named_scope("first%d" % n):
            for f in flavours:
                line = (first_at[f] + e) % side
                part[n, f] = mine[f, line] + from_sib[n, f]
                if e:
                    remote(
                        part.at[n, f], first_in.at[f, n], p_send.at[0], first_recv.at[f], along_first(f, e)
                    ).start()

    with jax.named_scope("tables"):
        high, low = split(cas_table())
        wide[0:SIDE, 0:SIDE] = high
        wide[0:SIDE, SIDE:] = low
        wide[SIDE:, 0:SIDE] = high
        wide[SIDE:, SIDE:] = low
        tall[0:SIDE, 0:SIDE] = high
        tall[0:SIDE, SIDE:] = high
        tall[SIDE:, 0:SIDE] = low
        tall[SIDE:, SIDE:] = low
        kern[...] = screen_kernel()

    own_line = len(steps)
    for f in flavours:
        with jax.named_scope("firstwait%d" % f):
            wait_all(first_in.at[f], first_recv.at[f])
        with jax.named_scope("second%d" % f):
            value = part[own_line, f]
            for n in range(len(steps)):
                value = value + first_in[f, n]
            summed[f] = value
            for n, e in enumerate(steps):
                remote(
                    summed.at[f], second_in.at[f, n], p_send.at[1], second_recv.at[f], along_second(f, e)
                ).start()
    for f in flavours:
        with jax.named_scope("secondwait%d" % f):
            wait_all(second_in.at[f], second_recv.at[f])
        with jax.named_scope("third%d" % f):
            value = summed[f]
            for n in range(len(steps)):
                value = value + second_in[f, n]
            line = first_at[f]
            vectors[f, line] = value
            for e in steps:
                remote(
                    vectors.at[f, line], vectors.at[f, line], p_send.at[2], third_recv.at[f], along_first(f, e)
                ).start()

    def back_copies(d):
        dy, dx = offs[d]
        to = device(at(dy, dx))
        here = dx * side + (my_y + dy) % side
        g = d // ROW_GROUP
        first = remote(quant.at[here], quant_in.at[d], q_send, q_recv.at[g], to)
        second = remote(scale.at[here], scale_in.at[d], s_send, s_recv.at[g], to)
        return first, second

    diagonal = lax.broadcasted_iota(jnp.int32, (points, SIDE), 0) == lax.broadcasted_iota(
        jnp.int32, (points, SIDE), 1
    )

    with jax.named_scope("gather"):
        to_sibling.wait()
        for f in flavours:
            wait_all(first_in.at[f], third_recv.at[f])

    for group in COLUMN_GROUPS:
        with jax.named_scope("pairs%d" % group[0]):
            size = len(group) * side
            lines = [(my_x + r) % side for r in group]
            low_half = jnp.concatenate([vectors[0, c].reshape(side * points, half) for c in lines], axis=0)
            high_half = jnp.concatenate([vectors[1, y, c] for c in lines for y in range(side)], axis=0)
            block = jnp.concatenate([low_half, high_half], axis=1)
            pair = jnp.concatenate(
                [jnp.dot(block, phi[h], preferred_element_type=F32) for h in range(2)], axis=1
            )
            peak = jnp.maximum(jnp.max(jnp.abs(pair), axis=1, keepdims=True), FLOOR)
            coded = jnp.round(pair * (TOP / peak)).astype(jnp.int32).astype(jnp.int16)
            step = jnp.broadcast_to(peak * (1.0 / TOP), (size * points, SIDE))
            for n, r in enumerate(group):
                for y in range(side):
                    rows = slice((n * side + y) * points, (n * side + y + 1) * points)
                    quant[r * side + y] = coded[rows]
                    scale[r * side + y] = jnp.sum(jnp.where(diagonal, step[rows], 0.0), axis=0, keepdims=True)
            for d in range(count):
                if offs[d][1] in group:
                    for copy in back_copies(d):
                        copy.start()

    rows = 2 * cells // SIDE

    def along(blocks):
        stacks = []
        for block, row_of, _ in blocks:
            step = jnp.sum(
                jnp.where(diagonal, jnp.broadcast_to(row_of, (points, SIDE)), 0.0), axis=1, keepdims=True
            )
            pair = block.astype(jnp.int32).astype(F32) * step
            square = pair * pair
            stacks.extend(square[:, r * SIDE : (r + 1) * SIDE] for r in range(rows))
        high, low = split(jnp.concatenate(stacks, axis=0))
        product = jnp.dot(jnp.concatenate([high, low], axis=1), wide[...], preferred_element_type=F32)
        product = product[:, :SIDE] + product[:, SIDE:]
        size = rows * points
        for n, (_, _, source) in enumerate(blocks):
            rows_done[pl.ds(pl.multiple_of(source * size, size), size), :] = product[n * size : (n + 1) * size]

    for g, start in enumerate(range(0, chips, ROW_GROUP)):
        size = min(ROW_GROUP, chips - start)
        with jax.named_scope("wait%d" % start):
            here = pl.ds(start, min(size, count - start))
            wait_all(quant_in.at[here], q_recv.at[g])
            wait_all(scale_in.at[here], s_recv.at[g])
        with jax.named_scope("along%d" % start):
            along([
                (quant_in[s], scale_in[s], at(-offs[s][0], -offs[s][1]))
                if s < count
                else (quant[my_y], scale[my_y], chip)
                for s in range(start, start + size)
            ])

    with jax.named_scope("across"):
        weight = jnp.concatenate([kern[...], kern[...]], axis=1)
        for first in range(0, points, 2):
            pieces = [rows_done[pl.ds(p, SIDE, stride=points), :] for p in (first, first + 1)]
            high, low = split(jnp.concatenate(pieces, axis=1))
            product = jnp.dot(tall[...], jnp.concatenate([high, low], axis=0), preferred_element_type=F32)
            high, low = split((product[:SIDE] + product[SIDE:]) * weight)
            middle[first // 2, 0:SIDE] = high
            middle[first // 2, SIDE:] = low
    with jax.named_scope("inverse"):
        for first in range(0, points, 2):
            product = jnp.dot(tall[...], middle[first // 2], preferred_element_type=F32)
            high, low = split(product[:SIDE] + product[SIDE:])
            for p in range(2):
                lanes = slice(p * SIDE, (p + 1) * SIDE)
                last[first + p, :, 0:SIDE] = high[:, lanes]
                last[first + p, :, SIDE:] = low[:, lanes]
    with jax.named_scope("sends"):
        wait_all(from_sib, sib_send)
        for n in range(3):
            wait_all(first_in, p_send.at[n])
        wait_all(quant_in, q_send)
        wait_all(scale_in, s_send)


def finish(last, wide, out_hbm, sheets, sem):
    points = last.shape[0]
    for first in range(0, points, 2):
        pair = pl.ds(first, 2)
        product = jnp.dot(last[pair].reshape(2 * SIDE, 2 * SIDE), wide[...], preferred_element_type=F32)
        sheets[pair] = (product[:, :SIDE] + product[:, SIDE:]).reshape(2, SIDE, SIDE)
        pltpu.make_async_copy(sheets.at[pair], out_hbm.at[pair], sem).start()
    pltpu.make_async_copy(sheets, out_hbm, sem).wait()


def shards(side, orbitals, point_index):
    orbital_count, cells = orbitals.shape
    chips = side * side
    points = point_index.shape[0] // (2 * chips)
    others = chips - 1
    half = orbital_count // 2
    dma = pltpu.SemaphoreType.DMA
    in_place = functools.partial(pltpu.with_memory_space_constraint, memory_space=pltpu.HBM)
    row_groups = pl.cdiv(chips, ROW_GROUP)
    last, wide = pl.pallas_call(
        functools.partial(body, side, points),
        out_shape=[
            jax.ShapeDtypeStruct((points, SIDE, 2 * SIDE), BF16),
            jax.ShapeDtypeStruct((2 * SIDE, 2 * SIDE), BF16),
        ],
        in_specs=[pl.BlockSpec(memory_space=pltpu.HBM)] * 2,
        out_specs=[pl.BlockSpec(memory_space=pltpu.VMEM)] * 2,
        scratch_shapes=[
            pltpu.VMEM((2, orbital_count, cells), BF16),
            pltpu.VMEM((1, point_index.shape[0]), jnp.int32),
            pltpu.VMEM((2, side, side, points, half), BF16),
            pltpu.VMEM((2, side, side, points, half), BF16),
            pltpu.VMEM((side, 2, side, points, half), BF16),
            pltpu.VMEM((side, 2, side, points, half), BF16),
            pltpu.VMEM((2, side - 1, side, points, half), BF16),
            pltpu.VMEM((2, side, points, half), BF16),
            pltpu.VMEM((2, side - 1, side, points, half), BF16),
            pltpu.VMEM((2, side, side, points, half), BF16),
            pltpu.VMEM((chips, points, 2 * cells), jnp.int16),
            pltpu.VMEM((chips, 1, SIDE), F32),
            pltpu.VMEM((others, points, 2 * cells), jnp.int16),
            pltpu.VMEM((others, 1, SIDE), F32),
            pltpu.VMEM((SIDE * points, SIDE), F32),
            pltpu.VMEM((2 * SIDE, 2 * SIDE), BF16),
            pltpu.VMEM((SIDE, SIDE), F32),
            pltpu.VMEM((points // 2, 2 * SIDE, 2 * SIDE), BF16),
            dma((2,)), dma, dma((side,)), dma, dma,
            dma((3,)), dma((2,)), dma((2,)), dma((2,)),
            dma, dma((row_groups,)), dma, dma((row_groups,)),
        ],
        compiler_params=pltpu.CompilerParams(
            collective_id=0, has_side_effects=True, vmem_limit_bytes=VMEM_BYTES
        ),
    )(in_place(orbitals), in_place(point_index.reshape(1, -1)))
    out = pl.pallas_call(
        finish,
        out_shape=jax.ShapeDtypeStruct((points, SIDE, SIDE), F32),
        in_specs=[pl.BlockSpec(memory_space=pltpu.VMEM)] * 2,
        out_specs=pl.BlockSpec(memory_space=pltpu.HBM),
        scratch_shapes=[pltpu.VMEM((points, SIDE, SIDE), F32), dma],
        compiler_params=pltpu.CompilerParams(vmem_limit_bytes=8 * 1024 * 1024),
    )(last, wide)
    return out[None]


def solution(mesh):
    grid_count = mesh.shape["grid"]
    size = math.isqrt(grid_count // 2)
    in_specs = (P(None, "grid"), P("pts"))
    out_specs = P("pts", "grid", None, None)
    step = functools.partial(shards, size)
    return jax.shard_map(step, mesh=mesh, in_specs=in_specs, out_specs=out_specs, check_vma=False)
```

```python
import functools
import math

import jax
import jax.numpy as jnp
from jax import lax
from jax.experimental import pallas as pl
from jax.experimental.pallas import tpu as pltpu
from jax.sharding import PartitionSpec as P

SIDE = 128
MESH = pl.DeviceIdType.MESH
F32 = jnp.float32
BF16 = jnp.bfloat16
TOP = 32766.0
FLOOR = 1e-30
REST_GROUPS = (6, 6)
VMEM_BYTES = 16 * 1024 * 1024


def split(values):
    high = values.astype(BF16)
    return high, (values - high.astype(F32)).astype(BF16)


def cas_table():
    rows = lax.broadcasted_iota(jnp.int32, (SIDE, SIDE), 0)
    columns = lax.broadcasted_iota(jnp.int32, (SIDE, SIDE), 1)
    angles = ((rows * columns) % SIDE).astype(F32) * (2.0 * math.pi / SIDE)
    return jnp.cos(angles) + jnp.sin(angles)


def screen_kernel():
    rows = lax.broadcasted_iota(jnp.int32, (SIDE, SIDE), 0)
    columns = lax.broadcasted_iota(jnp.int32, (SIDE, SIDE), 1)
    across = jnp.minimum(rows, SIDE - rows).astype(F32)
    along = jnp.minimum(columns, SIDE - columns).astype(F32)
    screening = SIDE / 16.0
    values = screening / jnp.sqrt(across * across + along * along + screening * screening)
    return jnp.where((rows == 0) & (columns == 0), 0.0, values * (1.0 / (SIDE * SIDE)))


def offsets(size_y, size_x):
    far = lambda d, n: min(d, n - d)
    every = [(dy, dx) for dy in range(size_y) for dx in range(size_x) if (dy, dx) != (0, 0)]
    return sorted(every, key=lambda o: (-far(o[0], size_y) - far(o[1], size_x), o))


def body(
    side, points,
    orb_hbm, idx_hbm, last, wide,
    phi, idx, mine, theirs, from_sib, part, first_in, summed, second_in, vectors, quant, scale, quant_in, scale_in,
    rows_done, tall, kern, middle,
    load_sem, sib_send, sib_recv, orb_send, orb_recv, p_send, first_recv, second_recv, third_recv,
    q_send, q_recv, s_send, s_recv,
):
    me = lax.axis_index("grid")
    core = me % 2
    chip = me // 2
    my_y = chip // side
    my_x = chip % side
    chips = side * side
    cells = phi.shape[2]
    orbital_count = phi.shape[1]
    part_points = points // 2
    offs = offsets(side, side)
    count = len(offs)
    steps = [2, 1, 3][-(side - 1) :]
    flavours = range(2)
    first_at = (my_x, my_y)
    second_at = (my_y, my_x)

    def at(dy, dx):
        return ((my_y + dy + side) % side) * side + (my_x + dx + side) % side

    def device(c):
        return {"grid": c * 2 + core}

    def along_first(f, e):
        return device(at(0, e) if f == 0 else at(e, 0))

    def along_second(f, e):
        return device(at(e, 0) if f == 0 else at(0, e))

    def remote(src, dst, send, recv, to):
        return pltpu.make_async_remote_copy(
            src_ref=src, dst_ref=dst, send_sem=send, recv_sem=recv, device_id=to, device_id_type=MESH
        )

    def wait_all(ref, sem):
        pltpu.make_async_copy(ref, ref, sem).wait()

    sibling = {"grid": chip * 2 + 1 - core}

    with jax.named_scope("signals"):
        load_idx = pltpu.make_async_copy(idx_hbm, idx, load_sem.at[1])
        load_idx.start()
        load_orb = pltpu.make_async_copy(orb_hbm, phi.at[core], load_sem.at[0])
        load_orb.start()
        barrier = pltpu.get_barrier_semaphore()
        pl.semaphore_signal(barrier, inc=1, device_id=sibling, device_id_type=MESH)
        for e in steps:
            for f in flavours:
                pl.semaphore_signal(barrier, inc=1, device_id=along_first(f, e), device_id_type=MESH)

    with jax.named_scope("indices"):
        load_idx.wait()
        total = idx.shape[1]
        column = jnp.transpose(jnp.broadcast_to(idx[...], (SIDE, total))) - me * cells
        column = column.reshape(chips, 2, points, SIDE)
        lane = lax.broadcasted_iota(jnp.int32, (chips * points, SIDE), 1)

    def owned(layer, to):
        chosen = jnp.where(layer == 0, column[:, 0], column[:, 1]).reshape(chips * points, SIDE)
        mask = jnp.concatenate(
            [jnp.where(chosen == lane + j * SIDE, 1.0, 0.0).astype(BF16) for j in range(cells // SIDE)], axis=1
        )
        found = lax.dot_general(mask, phi[core], (((1,), (1,)), ((), ())), preferred_element_type=F32)
        for y in range(side):
            for x in range(side):
                at_row = (y * side + x) * points
                to[0, x, y] = found[at_row : at_row + part_points].astype(BF16)
                to[1, y, x] = found[at_row + part_points : at_row + points].astype(BF16)

    with jax.named_scope("ownpicks"):
        load_orb.wait()
        owned(1 - core, theirs)

    with jax.named_scope("barrier"):
        pl.semaphore_wait(barrier, 2 * len(steps) + 1)

    with jax.named_scope("sibstart"):
        for n, e in enumerate(steps + [0]):
            for f in flavours:
                line = (first_at[f] + e) % side
                remote(theirs.at[f, line], from_sib.at[n, f], sib_send, sib_recv.at[n], sibling).start()
        to_sibling = remote(phi.at[core], phi.at[core], orb_send, orb_recv, sibling)
        to_sibling.start()
    with jax.named_scope("minepicks"):
        owned(core, mine)

    for n, e in enumerate(steps + [0]):
        with jax.named_scope("sibling%d" % n):
            wait_all(from_sib.at[n], sib_recv.at[n])
        with jax.named_scope("first%d" % n):
            for f in flavours:
                line = (first_at[f] + e) % side
                part[n, f] = mine[f, line] + from_sib[n, f]
                if e:
                    remote(
                        part.at[n, f], first_in.at[f, n], p_send.at[0], first_recv.at[f], along_first(f, e)
                    ).start()

    with jax.named_scope("tables"):
        high, low = split(cas_table())
        wide[0:SIDE, 0:SIDE] = high
        wide[0:SIDE, SIDE:] = low
        wide[SIDE:, 0:SIDE] = high
        wide[SIDE:, SIDE:] = low
        tall[0:SIDE, 0:SIDE] = high
        tall[0:SIDE, SIDE:] = high
        tall[SIDE:, 0:SIDE] = low
        tall[SIDE:, SIDE:] = low
        kern[...] = screen_kernel()

    own_line = len(steps)
    for f in flavours:
        with jax.named_scope("firstwait%d" % f):
            wait_all(first_in.at[f], first_recv.at[f])
        with jax.named_scope("second%d" % f):
            value = part[own_line, f]
            for n in range(len(steps)):
                value = value + first_in[f, n]
            summed[f] = value
            for n, e in enumerate(steps):
                remote(
                    summed.at[f], second_in.at[f, n], p_send.at[1], second_recv.at[f], along_second(f, e)
                ).start()
    for f in flavours:
        with jax.named_scope("secondwait%d" % f):
            wait_all(second_in.at[f], second_recv.at[f])
        with jax.named_scope("third%d" % f):
            value = summed[f]
            for n in range(len(steps)):
                value = value + second_in[f, n]
            line = first_at[f]
            vectors[f, line] = value
            for e in steps:
                remote(
                    vectors.at[f, line], vectors.at[f, line], p_send.at[2], third_recv.at[f], along_first(f, e)
                ).start()

    slots = [
        [o for o in offs if o[1 - f] == 0] + [o for o in offs if o[1 - f] != 0] for f in flavours
    ]
    sizes = (len(steps),) + REST_GROUPS
    bounds = [sum(sizes[:g]) for g in range(len(sizes) + 1)]

    def back_copies(f, g):
        copies = []
        for n in range(bounds[g], bounds[g + 1]):
            dy, dx = slots[f][n]
            line, place = ((dx, (my_y + dy) % side), (dy, (my_x + dx) % side))[f]
            to = device(at(dy, dx))
            copies.append(remote(scale.at[f, line, place], scale_in.at[f, n], s_send, s_recv.at[f, g], to))
            copies.append(remote(quant.at[f, line, place], quant_in.at[f, n], q_send, q_recv.at[f, g], to))
        return copies

    diagonal = lax.broadcasted_iota(jnp.int32, (part_points, SIDE), 0) == lax.broadcasted_iota(
        jnp.int32, (part_points, SIDE), 1
    )

    def pairs(f, lines):
        size = len(lines) * side * part_points
        block = jnp.concatenate(
            [vectors[f, (first_at[f] + r) % side].reshape(side * part_points, orbital_count) for r in lines], axis=0
        )
        pair = jnp.concatenate([jnp.dot(block, phi[h], preferred_element_type=F32) for h in range(2)], axis=1)
        peak = jnp.maximum(jnp.max(jnp.abs(pair), axis=1, keepdims=True), FLOOR)
        coded = jnp.round(pair * (TOP / peak)).astype(jnp.int32)
        step = jnp.broadcast_to(peak * (1.0 / TOP), (size, SIDE))
        for n, r in enumerate(lines):
            for place in range(side):
                rows = slice((n * side + place) * part_points, (n * side + place + 1) * part_points)
                quant[f, r, place] = coded[rows].astype(jnp.int16)
                scale[f, r, place] = jnp.sum(jnp.where(diagonal, step[rows], 0.0), axis=0, keepdims=True)

    to_sibling.wait()
    for f in flavours:
        with jax.named_scope("early%d" % f):
            pairs(f, [0])
            for copy in back_copies(f, 0):
                copy.start()
    for f in flavours:
        with jax.named_scope("gather%d" % f):
            wait_all(first_in.at[f], third_recv.at[f])
        with jax.named_scope("pairs%d" % f):
            pairs(f, steps)
            for g in range(1, len(sizes)):
                for copy in back_copies(f, g):
                    copy.start()

    rows = 2 * cells // SIDE

    def along(f, blocks):
        stacks = []
        for block, row_of, _ in blocks:
            step = jnp.sum(
                jnp.where(diagonal, jnp.broadcast_to(row_of, (part_points, SIDE)), 0.0), axis=1, keepdims=True
            )
            pair = block.astype(jnp.int32).astype(F32) * step
            square = pair * pair
            stacks.extend(square[:, r * SIDE : (r + 1) * SIDE] for r in range(rows))
        high, low = split(jnp.concatenate(stacks, axis=0))
        product = jnp.dot(jnp.concatenate([high, low], axis=1), wide[...], preferred_element_type=F32)
        product = product[:, :SIDE] + product[:, SIDE:]
        size = rows * part_points
        for n, (_, _, source) in enumerate(blocks):
            rows_done[f, pl.ds(pl.multiple_of(source * size, size), size), :] = product[n * size : (n + 1) * size]

    for f, g in [(0, 0), (1, 0)] + [(f, g) for f in flavours for g in range(1, len(sizes))]:
        group = range(bounds[g], bounds[g + 1])
        with jax.named_scope("wait%d%d" % (f, g)):
            wait_all(quant_in.at[f, pl.ds(bounds[g], sizes[g])], q_recv.at[f, g])
            wait_all(scale_in.at[f, pl.ds(bounds[g], sizes[g])], s_recv.at[f, g])
        with jax.named_scope("along%d%d" % (f, g)):
            blocks = [
                (quant_in[f, n], scale_in[f, n], at(-slots[f][n][0], -slots[f][n][1])) for n in group
            ]
            if g == 0:
                blocks.append((quant[f, 0, second_at[f]], scale[f, 0, second_at[f]], chip))
            along(f, blocks)

    with jax.named_scope("across"):
        weight = jnp.concatenate([kern[...], kern[...]], axis=1)
        for first in range(0, points, 2):
            pieces = [
                rows_done[p // part_points, pl.ds(p % part_points, SIDE, stride=part_points), :]
                for p in (first, first + 1)
            ]
            high, low = split(jnp.concatenate(pieces, axis=1))
            product = jnp.dot(tall[...], jnp.concatenate([high, low], axis=0), preferred_element_type=F32)
            high, low = split((product[:SIDE] + product[SIDE:]) * weight)
            middle[first // 2, 0:SIDE] = high
            middle[first // 2, SIDE:] = low
    with jax.named_scope("inverse"):
        for first in range(0, points, 2):
            product = jnp.dot(tall[...], middle[first // 2], preferred_element_type=F32)
            high, low = split(product[:SIDE] + product[SIDE:])
            for p in range(2):
                lanes = slice(p * SIDE, (p + 1) * SIDE)
                last[first + p, :, 0:SIDE] = high[:, lanes]
                last[first + p, :, SIDE:] = low[:, lanes]
    with jax.named_scope("sends"):
        wait_all(from_sib, sib_send)
        for n in range(3):
            wait_all(first_in, p_send.at[n])
        wait_all(quant_in, q_send)
        wait_all(scale_in, s_send)


def finish(last, wide, out_hbm, sheets, sem):
    points = last.shape[0]
    for first in range(0, points, 2):
        pair = pl.ds(first, 2)
        product = jnp.dot(last[pair].reshape(2 * SIDE, 2 * SIDE), wide[...], preferred_element_type=F32)
        sheets[pair] = (product[:, :SIDE] + product[:, SIDE:]).reshape(2, SIDE, SIDE)
        pltpu.make_async_copy(sheets.at[pair], out_hbm.at[pair], sem).start()
    pltpu.make_async_copy(sheets, out_hbm, sem).wait()


def shards(side, orbitals, point_index):
    orbital_count, cells = orbitals.shape
    chips = side * side
    points = point_index.shape[0] // (2 * chips)
    others = chips - 1
    part_points = points // 2
    dma = pltpu.SemaphoreType.DMA
    in_place = functools.partial(pltpu.with_memory_space_constraint, memory_space=pltpu.HBM)
    groups = 1 + len(REST_GROUPS)
    last, wide = pl.pallas_call(
        functools.partial(body, side, points),
        out_shape=[
            jax.ShapeDtypeStruct((points, SIDE, 2 * SIDE), BF16),
            jax.ShapeDtypeStruct((2 * SIDE, 2 * SIDE), BF16),
        ],
        in_specs=[pl.BlockSpec(memory_space=pltpu.HBM)] * 2,
        out_specs=[pl.BlockSpec(memory_space=pltpu.VMEM)] * 2,
        scratch_shapes=[
            pltpu.VMEM((2, orbital_count, cells), BF16),
            pltpu.VMEM((1, point_index.shape[0]), jnp.int32),
            pltpu.VMEM((2, side, side, part_points, orbital_count), BF16),
            pltpu.VMEM((2, side, side, part_points, orbital_count), BF16),
            pltpu.VMEM((side, 2, side, part_points, orbital_count), BF16),
            pltpu.VMEM((side, 2, side, part_points, orbital_count), BF16),
            pltpu.VMEM((2, side - 1, side, part_points, orbital_count), BF16),
            pltpu.VMEM((2, side, part_points, orbital_count), BF16),
            pltpu.VMEM((2, side - 1, side, part_points, orbital_count), BF16),
            pltpu.VMEM((2, side, side, part_points, orbital_count), BF16),
            pltpu.VMEM((2, side, side, part_points, 2 * cells), jnp.int16),
            pltpu.VMEM((2, side, side, 1, SIDE), F32),
            pltpu.VMEM((2, others, part_points, 2 * cells), jnp.int16),
            pltpu.VMEM((2, others, 1, SIDE), F32),
            pltpu.VMEM((2, SIDE * part_points, SIDE), F32),
            pltpu.VMEM((2 * SIDE, 2 * SIDE), BF16),
            pltpu.VMEM((SIDE, SIDE), F32),
            pltpu.VMEM((points // 2, 2 * SIDE, 2 * SIDE), BF16),
            dma((2,)), dma, dma((side,)), dma, dma,
            dma((3,)), dma((2,)), dma((2,)), dma((2,)),
            dma, dma((2, groups)), dma, dma((2, groups)),
        ],
        compiler_params=pltpu.CompilerParams(
            collective_id=0, has_side_effects=True, vmem_limit_bytes=VMEM_BYTES
        ),
    )(in_place(orbitals), in_place(point_index.reshape(1, -1)))
    out = pl.pallas_call(
        finish,
        out_shape=jax.ShapeDtypeStruct((points, SIDE, SIDE), F32),
        in_specs=[pl.BlockSpec(memory_space=pltpu.VMEM)] * 2,
        out_specs=pl.BlockSpec(memory_space=pltpu.HBM),
        scratch_shapes=[pltpu.VMEM((points, SIDE, SIDE), F32), dma],
        compiler_params=pltpu.CompilerParams(vmem_limit_bytes=8 * 1024 * 1024),
    )(last, wide)
    return out[None]


def solution(mesh):
    grid_count = mesh.shape["grid"]
    size = math.isqrt(grid_count // 2)
    in_specs = (P(None, "grid"), P("pts"))
    out_specs = P("pts", "grid", None, None)
    step = functools.partial(shards, size)
    return jax.shard_map(step, mesh=mesh, in_specs=in_specs, out_specs=out_specs, check_vma=False)
```

```python
import functools
import math

import jax
import jax.numpy as jnp
from jax import lax
from jax.experimental import pallas as pl
from jax.experimental.pallas import tpu as pltpu
from jax.sharding import PartitionSpec as P

SIDE = 128
MESH = pl.DeviceIdType.MESH
F32 = jnp.float32
BF16 = jnp.bfloat16
TOP = 32766.0
FLOOR = 1e-30
REST_GROUPS = (12,)
VMEM_BYTES = 16 * 1024 * 1024


def split(values):
    high = values.astype(BF16)
    return high, (values - high.astype(F32)).astype(BF16)


def cas_table():
    rows = lax.broadcasted_iota(jnp.int32, (SIDE, SIDE), 0)
    columns = lax.broadcasted_iota(jnp.int32, (SIDE, SIDE), 1)
    angles = ((rows * columns) % SIDE).astype(F32) * (2.0 * math.pi / SIDE)
    return jnp.cos(angles) + jnp.sin(angles)


def screen_kernel():
    rows = lax.broadcasted_iota(jnp.int32, (SIDE, SIDE), 0)
    columns = lax.broadcasted_iota(jnp.int32, (SIDE, SIDE), 1)
    across = jnp.minimum(rows, SIDE - rows).astype(F32)
    along = jnp.minimum(columns, SIDE - columns).astype(F32)
    screening = SIDE / 16.0
    values = screening / jnp.sqrt(across * across + along * along + screening * screening)
    return jnp.where((rows == 0) & (columns == 0), 0.0, values * (1.0 / (SIDE * SIDE)))


def offsets(size_y, size_x):
    far = lambda d, n: min(d, n - d)
    every = [(dy, dx) for dy in range(size_y) for dx in range(size_x) if (dy, dx) != (0, 0)]
    return sorted(every, key=lambda o: (-far(o[0], size_y) - far(o[1], size_x), o))


def body(
    side, points,
    orb_hbm, idx_hbm, done, last, wide,
    phi, idx, their_mask, mine, theirs, from_sib, part, first_in, summed, second_in, vectors, quant, scale, quant_in, scale_in,
    rows_done, tall, kern, middle, first_last,
    load_sem, sib_send, sib_recv, orb_send, orb_recv, p_send, first_recv, second_recv, third_recv,
    q_send, q_recv, s_send, s_recv,
):
    me = lax.axis_index("grid")
    core = me % 2
    chip = me // 2
    my_y = chip // side
    my_x = chip % side
    chips = side * side
    cells = phi.shape[2]
    orbital_count = phi.shape[1]
    part_points = points // 2
    offs = offsets(side, side)
    count = len(offs)
    steps = [2, 1, 3][-(side - 1) :]
    flavours = range(2)
    first_at = (my_x, my_y)
    second_at = (my_y, my_x)

    def at(dy, dx):
        return ((my_y + dy + side) % side) * side + (my_x + dx + side) % side

    def device(c):
        return {"grid": c * 2 + core}

    def along_first(f, e):
        return device(at(0, e) if f == 0 else at(e, 0))

    def along_second(f, e):
        return device(at(e, 0) if f == 0 else at(0, e))

    def remote(src, dst, send, recv, to):
        return pltpu.make_async_remote_copy(
            src_ref=src, dst_ref=dst, send_sem=send, recv_sem=recv, device_id=to, device_id_type=MESH
        )

    def wait_all(ref, sem):
        pltpu.make_async_copy(ref, ref, sem).wait()

    sibling = {"grid": chip * 2 + 1 - core}

    with jax.named_scope("signals"):
        load_idx = pltpu.make_async_copy(idx_hbm, idx, load_sem.at[1])
        load_idx.start()
        load_orb = pltpu.make_async_copy(orb_hbm, phi.at[core], load_sem.at[0])
        load_orb.start()
        barrier = pltpu.get_barrier_semaphore()
        pl.semaphore_signal(barrier, inc=1, device_id=sibling, device_id_type=MESH)
        for e in steps:
            for f in flavours:
                pl.semaphore_signal(barrier, inc=1, device_id=along_first(f, e), device_id_type=MESH)

    with jax.named_scope("indices"):
        load_idx.wait()
        total = idx.shape[1]
        column = jnp.transpose(jnp.broadcast_to(idx[...], (SIDE, total))) - me * cells
        column = column.reshape(chips, 2, points, SIDE)
        lane = lax.broadcasted_iota(jnp.int32, (chips * points, SIDE), 1)

    def mask_of(layer):
        chosen = jnp.where(layer == 0, column[:, 0], column[:, 1]).reshape(chips * points, SIDE)
        return jnp.concatenate(
            [jnp.where(chosen == lane + j * SIDE, 1.0, 0.0).astype(BF16) for j in range(cells // SIDE)], axis=1
        )

    def owned(mask, to):
        found = lax.dot_general(mask, phi[core], (((1,), (1,)), ((), ())), preferred_element_type=F32)
        for y in range(side):
            for x in range(side):
                at_row = (y * side + x) * points
                to[0, x, y] = found[at_row : at_row + part_points].astype(BF16)
                to[1, y, x] = found[at_row + part_points : at_row + points].astype(BF16)

    with jax.named_scope("ownpicks"):
        their_mask[...] = mask_of(1 - core)
        load_orb.wait()
        owned(their_mask[...], theirs)

    with jax.named_scope("barrier"):
        pl.semaphore_wait(barrier, 2 * len(steps) + 1)

    with jax.named_scope("sibstart"):
        for n, e in enumerate(steps + [0]):
            for f in flavours:
                line = (first_at[f] + e) % side
                remote(theirs.at[f, line], from_sib.at[n, f], sib_send, sib_recv.at[n], sibling).start()
        to_sibling = remote(phi.at[core], phi.at[core], orb_send, orb_recv, sibling)
        to_sibling.start()
    with jax.named_scope("minepicks"):
        owned(mask_of(core), mine)

    for n, e in enumerate(steps + [0]):
        with jax.named_scope("sibling%d" % n):
            wait_all(from_sib.at[n], sib_recv.at[n])
        with jax.named_scope("first%d" % n):
            for f in flavours:
                line = (first_at[f] + e) % side
                part[n, f] = mine[f, line] + from_sib[n, f]
                if e:
                    remote(
                        part.at[n, f], first_in.at[f, n], p_send.at[0], first_recv.at[f], along_first(f, e)
                    ).start()

    with jax.named_scope("tables"):
        high, low = split(cas_table())
        wide[0:SIDE, 0:SIDE] = high
        wide[0:SIDE, SIDE:] = low
        wide[SIDE:, 0:SIDE] = high
        wide[SIDE:, SIDE:] = low
        tall[0:SIDE, 0:SIDE] = high
        tall[0:SIDE, SIDE:] = high
        tall[SIDE:, 0:SIDE] = low
        tall[SIDE:, SIDE:] = low
        kern[...] = screen_kernel()

    own_line = len(steps)
    for f in flavours:
        with jax.named_scope("firstwait%d" % f):
            wait_all(first_in.at[f], first_recv.at[f])
        with jax.named_scope("second%d" % f):
            value = part[own_line, f]
            for n in range(len(steps)):
                value = value + first_in[f, n]
            summed[f] = value
            for n, e in enumerate(steps):
                remote(
                    summed.at[f], second_in.at[f, n], p_send.at[1], second_recv.at[f], along_second(f, e)
                ).start()
    for f in flavours:
        with jax.named_scope("secondwait%d" % f):
            wait_all(second_in.at[f], second_recv.at[f])
        with jax.named_scope("third%d" % f):
            value = summed[f]
            for n in range(len(steps)):
                value = value + second_in[f, n]
            line = first_at[f]
            vectors[f, line] = value
            for e in steps:
                remote(
                    vectors.at[f, line], vectors.at[f, line], p_send.at[2], third_recv.at[f], along_first(f, e)
                ).start()

    slots = [
        [o for o in offs if o[1 - f] == 0] + [o for o in offs if o[1 - f] != 0] for f in flavours
    ]
    sizes = (len(steps),) + REST_GROUPS
    bounds = [sum(sizes[:g]) for g in range(len(sizes) + 1)]

    def back_copies(f, g):
        copies = []
        for n in range(bounds[g], bounds[g + 1]):
            dy, dx = slots[f][n]
            line, place = ((dx, (my_y + dy) % side), (dy, (my_x + dx) % side))[f]
            to = device(at(dy, dx))
            copies.append(remote(scale.at[f, line, place], scale_in.at[f, n], s_send, s_recv.at[f, g], to))
            copies.append(remote(quant.at[f, line, place], quant_in.at[f, n], q_send, q_recv.at[f, g], to))
        return copies

    diagonal = lax.broadcasted_iota(jnp.int32, (part_points, SIDE), 0) == lax.broadcasted_iota(
        jnp.int32, (part_points, SIDE), 1
    )

    def pairs(f, lines):
        size = len(lines) * side * part_points
        block = jnp.concatenate(
            [vectors[f, (first_at[f] + r) % side].reshape(side * part_points, orbital_count) for r in lines], axis=0
        )
        pair = jnp.concatenate([jnp.dot(block, phi[h], preferred_element_type=F32) for h in range(2)], axis=1)
        peak = jnp.maximum(jnp.max(jnp.abs(pair), axis=1, keepdims=True), FLOOR)
        coded = jnp.round(pair * (TOP / peak)).astype(jnp.int32)
        step = jnp.broadcast_to(peak * (1.0 / TOP), (size, SIDE))
        for n, r in enumerate(lines):
            for place in range(side):
                rows = slice((n * side + place) * part_points, (n * side + place + 1) * part_points)
                quant[f, r, place] = coded[rows].astype(jnp.int16)
                scale[f, r, place] = jnp.sum(jnp.where(diagonal, step[rows], 0.0), axis=0, keepdims=True)

    to_sibling.wait()
    for f in flavours:
        with jax.named_scope("early%d" % f):
            pairs(f, [0])
            for copy in back_copies(f, 0):
                copy.start()
    for f in flavours:
        with jax.named_scope("gather%d" % f):
            wait_all(first_in.at[f], third_recv.at[f])
        with jax.named_scope("pairs%d" % f):
            pairs(f, steps)
            for g in range(1, len(sizes)):
                for copy in back_copies(f, g):
                    copy.start()

    rows = 2 * cells // SIDE

    def along(f, blocks):
        stacks = []
        for block, row_of, _ in blocks:
            step = jnp.sum(
                jnp.where(diagonal, jnp.broadcast_to(row_of, (part_points, SIDE)), 0.0), axis=1, keepdims=True
            )
            pair = block.astype(jnp.int32).astype(F32) * step
            square = pair * pair
            stacks.extend(square[:, r * SIDE : (r + 1) * SIDE] for r in range(rows))
        high, low = split(jnp.concatenate(stacks, axis=0))
        product = jnp.dot(jnp.concatenate([high, low], axis=1), wide[...], preferred_element_type=F32)
        product = product[:, :SIDE] + product[:, SIDE:]
        size = rows * part_points
        for n, (_, _, source) in enumerate(blocks):
            rows_done[f, pl.ds(pl.multiple_of(source * size, size), size), :] = product[n * size : (n + 1) * size]

    def across(f):
        weight = jnp.concatenate([kern[...], kern[...]], axis=1)
        for n in range(part_points // 2):
            pieces = [rows_done[f, pl.ds(p, SIDE, stride=part_points), :] for p in (2 * n, 2 * n + 1)]
            high, low = split(jnp.concatenate(pieces, axis=1))
            product = jnp.dot(tall[...], jnp.concatenate([high, low], axis=0), preferred_element_type=F32)
            high, low = split((product[:SIDE] + product[SIDE:]) * weight)
            middle[f, n, 0:SIDE] = high
            middle[f, n, SIDE:] = low
        for n in range(part_points // 2):
            product = jnp.dot(tall[...], middle[f, n], preferred_element_type=F32)
            high, low = split(product[:SIDE] + product[SIDE:])
            for p in range(2):
                lanes = slice(p * SIDE, (p + 1) * SIDE)
                to = (first_last, last)[f]
                to[2 * n + p, :, 0:SIDE] = high[:, lanes]
                to[2 * n + p, :, SIDE:] = low[:, lanes]

    for f, g in [(0, 0), (1, 0)] + [(f, g) for f in flavours for g in range(1, len(sizes))]:
        group = range(bounds[g], bounds[g + 1])
        with jax.named_scope("wait%d%d" % (f, g)):
            wait_all(quant_in.at[f, pl.ds(bounds[g], sizes[g])], q_recv.at[f, g])
            wait_all(scale_in.at[f, pl.ds(bounds[g], sizes[g])], s_recv.at[f, g])
        with jax.named_scope("along%d%d" % (f, g)):
            blocks = [
                (quant_in[f, n], scale_in[f, n], at(-slots[f][n][0], -slots[f][n][1])) for n in group
            ]
            if g == 0:
                blocks.append((quant[f, 0, second_at[f]], scale[f, 0, second_at[f]], chip))
            along(f, blocks)
        if g == len(sizes) - 1:
            with jax.named_scope("across%d" % f):
                across(f)
            if f == 0:
                with jax.named_scope("output"):
                    for first in range(0, part_points, 2):
                        done[first : first + 2] = last_product(first_last[first : first + 2], wide[...])

    with jax.named_scope("sends"):
        wait_all(from_sib, sib_send)
        for n in range(3):
            wait_all(first_in, p_send.at[n])
        wait_all(quant_in, q_send)
        wait_all(scale_in, s_send)


def last_product(values, wide):
    count = values.shape[0]
    product = jnp.dot(values.reshape(count * SIDE, 2 * SIDE), wide, preferred_element_type=F32)
    return (product[:, :SIDE] + product[:, SIDE:]).reshape(count, SIDE, SIDE)


def finish(done, last, wide, out_hbm, sheets, sem):
    ready = done.shape[0]
    pltpu.make_async_copy(done, out_hbm.at[pl.ds(0, ready)], sem).start()
    for first in range(0, last.shape[0], 2):
        sheets[first : first + 2] = last_product(last[first : first + 2], wide[...])
        pltpu.make_async_copy(
            sheets.at[pl.ds(first, 2)], out_hbm.at[pl.ds(ready + first, 2)], sem
        ).start()
    pltpu.make_async_copy(out_hbm, out_hbm, sem).wait()


def shards(side, orbitals, point_index):
    orbital_count, cells = orbitals.shape
    chips = side * side
    points = point_index.shape[0] // (2 * chips)
    others = chips - 1
    part_points = points // 2
    dma = pltpu.SemaphoreType.DMA
    in_place = functools.partial(pltpu.with_memory_space_constraint, memory_space=pltpu.HBM)
    groups = 1 + len(REST_GROUPS)
    done, last, wide = pl.pallas_call(
        functools.partial(body, side, points),
        out_shape=[
            jax.ShapeDtypeStruct((part_points, SIDE, SIDE), F32),
            jax.ShapeDtypeStruct((part_points, SIDE, 2 * SIDE), BF16),
            jax.ShapeDtypeStruct((2 * SIDE, 2 * SIDE), BF16),
        ],
        in_specs=[pl.BlockSpec(memory_space=pltpu.HBM)] * 2,
        out_specs=[pl.BlockSpec(memory_space=pltpu.VMEM)] * 3,
        scratch_shapes=[
            pltpu.VMEM((2, orbital_count, cells), BF16),
            pltpu.VMEM((1, point_index.shape[0]), jnp.int32),
            pltpu.VMEM((chips * points, cells), BF16),
            pltpu.VMEM((2, side, side, part_points, orbital_count), BF16),
            pltpu.VMEM((2, side, side, part_points, orbital_count), BF16),
            pltpu.VMEM((side, 2, side, part_points, orbital_count), BF16),
            pltpu.VMEM((side, 2, side, part_points, orbital_count), BF16),
            pltpu.VMEM((2, side - 1, side, part_points, orbital_count), BF16),
            pltpu.VMEM((2, side, part_points, orbital_count), BF16),
            pltpu.VMEM((2, side - 1, side, part_points, orbital_count), BF16),
            pltpu.VMEM((2, side, side, part_points, orbital_count), BF16),
            pltpu.VMEM((2, side, side, part_points, 2 * cells), jnp.int16),
            pltpu.VMEM((2, side, side, 1, SIDE), F32),
            pltpu.VMEM((2, others, part_points, 2 * cells), jnp.int16),
            pltpu.VMEM((2, others, 1, SIDE), F32),
            pltpu.VMEM((2, SIDE * part_points, SIDE), F32),
            pltpu.VMEM((2 * SIDE, 2 * SIDE), BF16),
            pltpu.VMEM((SIDE, SIDE), F32),
            pltpu.VMEM((2, part_points // 2, 2 * SIDE, 2 * SIDE), BF16),
            pltpu.VMEM((part_points, SIDE, 2 * SIDE), BF16),
            dma((2,)), dma, dma((side,)), dma, dma,
            dma((3,)), dma((2,)), dma((2,)), dma((2,)),
            dma, dma((2, groups)), dma, dma((2, groups)),
        ],
        compiler_params=pltpu.CompilerParams(
            collective_id=0, has_side_effects=True, vmem_limit_bytes=VMEM_BYTES
        ),
    )(in_place(orbitals), in_place(point_index.reshape(1, -1)))
    out = pl.pallas_call(
        finish,
        out_shape=jax.ShapeDtypeStruct((points, SIDE, SIDE), F32),
        in_specs=[pl.BlockSpec(memory_space=pltpu.VMEM)] * 3,
        out_specs=pl.BlockSpec(memory_space=pltpu.HBM),
        scratch_shapes=[pltpu.VMEM((part_points, SIDE, SIDE), F32), dma],
        compiler_params=pltpu.CompilerParams(vmem_limit_bytes=8 * 1024 * 1024),
    )(done, last, wide)
    return out[None]


def solution(mesh):
    grid_count = mesh.shape["grid"]
    size = math.isqrt(grid_count // 2)
    in_specs = (P(None, "grid"), P("pts"))
    out_specs = P("pts", "grid", None, None)
    step = functools.partial(shards, size)
    return jax.shard_map(step, mesh=mesh, in_specs=in_specs, out_specs=out_specs, check_vma=False)
```

```python
import functools
import math

import jax
import jax.numpy as jnp
from jax import lax
from jax.experimental import pallas as pl
from jax.experimental.pallas import tpu as pltpu
from jax.sharding import PartitionSpec as P

SIDE = 128
MESH = pl.DeviceIdType.MESH
F32 = jnp.float32
BF16 = jnp.bfloat16
TOP = 32766.0
FLOOR = 1e-30
REST_GROUPS = (12,)
VMEM_BYTES = 16 * 1024 * 1024


def split(values):
    high = values.astype(BF16)
    return high, (values - high.astype(F32)).astype(BF16)


def cas_table():
    rows = lax.broadcasted_iota(jnp.int32, (SIDE, SIDE), 0)
    columns = lax.broadcasted_iota(jnp.int32, (SIDE, SIDE), 1)
    angles = ((rows * columns) % SIDE).astype(F32) * (2.0 * math.pi / SIDE)
    return jnp.cos(angles) + jnp.sin(angles)


def screen_kernel():
    rows = lax.broadcasted_iota(jnp.int32, (SIDE, SIDE), 0)
    columns = lax.broadcasted_iota(jnp.int32, (SIDE, SIDE), 1)
    across = jnp.minimum(rows, SIDE - rows).astype(F32)
    along = jnp.minimum(columns, SIDE - columns).astype(F32)
    screening = SIDE / 16.0
    values = screening / jnp.sqrt(across * across + along * along + screening * screening)
    return jnp.where((rows == 0) & (columns == 0), 0.0, values * (1.0 / (SIDE * SIDE)))


def offsets(size_y, size_x):
    far = lambda d, n: min(d, n - d)
    every = [(dy, dx) for dy in range(size_y) for dx in range(size_x) if (dy, dx) != (0, 0)]
    return sorted(every, key=lambda o: (-far(o[0], size_y) - far(o[1], size_x), o))


def body(
    side, points,
    orb_hbm, idx_hbm, done, last, wide,
    phi, idx, their_mask, mine, theirs, from_sib, part, first_in, summed, second_in, vectors, quant, scale, quant_in, scale_in,
    rows_done, tall, kern, middle, first_last,
    load_sem, sib_send, sib_recv, orb_send, orb_recv, p_send, first_recv, second_recv, third_recv,
    q_send, q_recv, s_send, s_recv,
):
    me = lax.axis_index("grid")
    core = me % 2
    chip = me // 2
    my_y = chip // side
    my_x = chip % side
    chips = side * side
    cells = phi.shape[2]
    orbital_count = phi.shape[1]
    part_points = points // 2
    offs = offsets(side, side)
    count = len(offs)
    steps = [2, 1, 3][-(side - 1) :]
    flavours = range(2)
    first_at = (my_x, my_y)
    second_at = (my_y, my_x)

    def at(dy, dx):
        return ((my_y + dy + side) % side) * side + (my_x + dx + side) % side

    def device(c):
        return {"grid": c * 2 + core}

    def along_first(f, e):
        return device(at(0, e) if f == 0 else at(e, 0))

    def along_second(f, e):
        return device(at(e, 0) if f == 0 else at(0, e))

    def remote(src, dst, send, recv, to):
        return pltpu.make_async_remote_copy(
            src_ref=src, dst_ref=dst, send_sem=send, recv_sem=recv, device_id=to, device_id_type=MESH
        )

    def wait_all(ref, sem):
        pltpu.make_async_copy(ref, ref, sem).wait()

    sibling = {"grid": chip * 2 + 1 - core}

    with jax.named_scope("signals"):
        load_idx = pltpu.make_async_copy(idx_hbm, idx, load_sem.at[1])
        load_idx.start()
        load_orb = pltpu.make_async_copy(orb_hbm, phi.at[core], load_sem.at[0])
        load_orb.start()
        barrier = pltpu.get_barrier_semaphore()
        pl.semaphore_signal(barrier, inc=1, device_id=sibling, device_id_type=MESH)
        for e in steps:
            for f in flavours:
                pl.semaphore_signal(barrier, inc=1, device_id=along_first(f, e), device_id_type=MESH)

    with jax.named_scope("indices"):
        load_idx.wait()
        total = idx.shape[1]
        column = jnp.transpose(jnp.broadcast_to(idx[...], (SIDE, total))) - me * cells
        column = column.reshape(chips, 2, points, SIDE)
        lane = lax.broadcasted_iota(jnp.int32, (chips * points, SIDE), 1)

    def mask_of(layer):
        chosen = jnp.where(layer == 0, column[:, 0], column[:, 1]).reshape(chips * points, SIDE)
        return jnp.concatenate(
            [jnp.where(chosen == lane + j * SIDE, 1.0, 0.0).astype(BF16) for j in range(cells // SIDE)], axis=1
        )

    def owned(mask, to):
        found = lax.dot_general(mask, phi[core], (((1,), (1,)), ((), ())), preferred_element_type=F32)
        for y in range(side):
            for x in range(side):
                at_row = (y * side + x) * points
                to[0, x, y] = found[at_row : at_row + part_points].astype(BF16)
                to[1, y, x] = found[at_row + part_points : at_row + points].astype(BF16)

    with jax.named_scope("ownpicks"):
        their_mask[...] = mask_of(1 - core)
        load_orb.wait()
        owned(their_mask[...], theirs)

    with jax.named_scope("barrier"):
        pl.semaphore_wait(barrier, 2 * len(steps) + 1)

    with jax.named_scope("sibstart"):
        for n, e in enumerate(steps + [0]):
            for f in flavours:
                line = (first_at[f] + e) % side
                remote(theirs.at[f, line], from_sib.at[n, f], sib_send, sib_recv.at[n], sibling).start()
    with jax.named_scope("minepicks"):
        owned(mask_of(core), mine)

    for n, e in enumerate(steps + [0]):
        with jax.named_scope("sibling%d" % n):
            wait_all(from_sib.at[n], sib_recv.at[n])
        with jax.named_scope("first%d" % n):
            for f in flavours:
                line = (first_at[f] + e) % side
                part[n, f] = mine[f, line] + from_sib[n, f]
                if e:
                    remote(
                        part.at[n, f], first_in.at[f, n], p_send.at[0], first_recv.at[f], along_first(f, e)
                    ).start()

    to_sibling = remote(phi.at[core], phi.at[core], orb_send, orb_recv, sibling)
    to_sibling.start()

    with jax.named_scope("tables"):
        high, low = split(cas_table())
        wide[0:SIDE, 0:SIDE] = high
        wide[0:SIDE, SIDE:] = low
        wide[SIDE:, 0:SIDE] = high
        wide[SIDE:, SIDE:] = low
        tall[0:SIDE, 0:SIDE] = high
        tall[0:SIDE, SIDE:] = high
        tall[SIDE:, 0:SIDE] = low
        tall[SIDE:, SIDE:] = low
        kern[...] = screen_kernel()

    own_line = len(steps)
    for f in flavours:
        with jax.named_scope("firstwait%d" % f):
            wait_all(first_in.at[f], first_recv.at[f])
        with jax.named_scope("second%d" % f):
            value = part[own_line, f]
            for n in range(len(steps)):
                value = value + first_in[f, n]
            summed[f] = value
            for n, e in enumerate(steps):
                remote(
                    summed.at[f], second_in.at[f, n], p_send.at[1], second_recv.at[f], along_second(f, e)
                ).start()
    for f in flavours:
        with jax.named_scope("secondwait%d" % f):
            wait_all(second_in.at[f], second_recv.at[f])
        with jax.named_scope("third%d" % f):
            value = summed[f]
            for n in range(len(steps)):
                value = value + second_in[f, n]
            line = first_at[f]
            vectors[f, line] = value
            for e in steps:
                remote(
                    vectors.at[f, line], vectors.at[f, line], p_send.at[2], third_recv.at[f], along_first(f, e)
                ).start()

    slots = [
        [o for o in offs if o[1 - f] == 0] + [o for o in offs if o[1 - f] != 0] for f in flavours
    ]
    sizes = (len(steps),) + REST_GROUPS
    bounds = [sum(sizes[:g]) for g in range(len(sizes) + 1)]

    def back_copies(f, g):
        copies = []
        for n in range(bounds[g], bounds[g + 1]):
            dy, dx = slots[f][n]
            line, place = ((dx, (my_y + dy) % side), (dy, (my_x + dx) % side))[f]
            to = device(at(dy, dx))
            copies.append(remote(scale.at[f, line, place], scale_in.at[f, n], s_send, s_recv.at[f, g], to))
            copies.append(remote(quant.at[f, line, place], quant_in.at[f, n], q_send, q_recv.at[f, g], to))
        return copies

    diagonal = lax.broadcasted_iota(jnp.int32, (part_points, SIDE), 0) == lax.broadcasted_iota(
        jnp.int32, (part_points, SIDE), 1
    )

    def pairs(f, lines):
        size = len(lines) * side * part_points
        block = jnp.concatenate(
            [vectors[f, (first_at[f] + r) % side].reshape(side * part_points, orbital_count) for r in lines], axis=0
        )
        pair = jnp.concatenate([jnp.dot(block, phi[h], preferred_element_type=F32) for h in range(2)], axis=1)
        peak = jnp.maximum(jnp.max(jnp.abs(pair), axis=1, keepdims=True), FLOOR)
        coded = jnp.round(pair * (TOP / peak)).astype(jnp.int32)
        step = jnp.broadcast_to(peak * (1.0 / TOP), (size, SIDE))
        for n, r in enumerate(lines):
            for place in range(side):
                rows = slice((n * side + place) * part_points, (n * side + place + 1) * part_points)
                quant[f, r, place] = coded[rows].astype(jnp.int16)
                scale[f, r, place] = jnp.sum(jnp.where(diagonal, step[rows], 0.0), axis=0, keepdims=True)

    to_sibling.wait()
    for f in flavours:
        with jax.named_scope("early%d" % f):
            pairs(f, [0])
            for copy in back_copies(f, 0):
                copy.start()
    for f in flavours:
        with jax.named_scope("gather%d" % f):
            wait_all(first_in.at[f], third_recv.at[f])
        with jax.named_scope("pairs%d" % f):
            pairs(f, steps)
            for g in range(1, len(sizes)):
                for copy in back_copies(f, g):
                    copy.start()

    rows = 2 * cells // SIDE

    def along(f, blocks):
        stacks = []
        for block, row_of, _ in blocks:
            step = jnp.sum(
                jnp.where(diagonal, jnp.broadcast_to(row_of, (part_points, SIDE)), 0.0), axis=1, keepdims=True
            )
            pair = block.astype(jnp.int32).astype(F32) * step
            square = pair * pair
            stacks.extend(square[:, r * SIDE : (r + 1) * SIDE] for r in range(rows))
        high, low = split(jnp.concatenate(stacks, axis=0))
        product = jnp.dot(jnp.concatenate([high, low], axis=1), wide[...], preferred_element_type=F32)
        product = product[:, :SIDE] + product[:, SIDE:]
        size = rows * part_points
        for n, (_, _, source) in enumerate(blocks):
            rows_done[f, pl.ds(pl.multiple_of(source * size, size), size), :] = product[n * size : (n + 1) * size]

    def across(f):
        weight = jnp.concatenate([kern[...], kern[...]], axis=1)
        for n in range(part_points // 2):
            pieces = [rows_done[f, pl.ds(p, SIDE, stride=part_points), :] for p in (2 * n, 2 * n + 1)]
            high, low = split(jnp.concatenate(pieces, axis=1))
            product = jnp.dot(tall[...], jnp.concatenate([high, low], axis=0), preferred_element_type=F32)
            high, low = split((product[:SIDE] + product[SIDE:]) * weight)
            middle[f, n, 0:SIDE] = high
            middle[f, n, SIDE:] = low
        for n in range(part_points // 2):
            product = jnp.dot(tall[...], middle[f, n], preferred_element_type=F32)
            high, low = split(product[:SIDE] + product[SIDE:])
            for p in range(2):
                lanes = slice(p * SIDE, (p + 1) * SIDE)
                to = (first_last, last)[f]
                to[2 * n + p, :, 0:SIDE] = high[:, lanes]
                to[2 * n + p, :, SIDE:] = low[:, lanes]

    for f, g in [(0, 0), (1, 0)] + [(f, g) for f in flavours for g in range(1, len(sizes))]:
        group = range(bounds[g], bounds[g + 1])
        with jax.named_scope("wait%d%d" % (f, g)):
            wait_all(quant_in.at[f, pl.ds(bounds[g], sizes[g])], q_recv.at[f, g])
            wait_all(scale_in.at[f, pl.ds(bounds[g], sizes[g])], s_recv.at[f, g])
        with jax.named_scope("along%d%d" % (f, g)):
            blocks = [
                (quant_in[f, n], scale_in[f, n], at(-slots[f][n][0], -slots[f][n][1])) for n in group
            ]
            if g == 0:
                blocks.append((quant[f, 0, second_at[f]], scale[f, 0, second_at[f]], chip))
            along(f, blocks)
        if g == len(sizes) - 1:
            with jax.named_scope("across%d" % f):
                across(f)
            if f == 0:
                with jax.named_scope("output"):
                    for first in range(0, part_points, 2):
                        done[first : first + 2] = last_product(first_last[first : first + 2], wide[...])

    with jax.named_scope("sends"):
        wait_all(from_sib, sib_send)
        for n in range(3):
            wait_all(first_in, p_send.at[n])
        wait_all(quant_in, q_send)
        wait_all(scale_in, s_send)


def last_product(values, wide):
    count = values.shape[0]
    product = jnp.dot(values.reshape(count * SIDE, 2 * SIDE), wide, preferred_element_type=F32)
    return (product[:, :SIDE] + product[:, SIDE:]).reshape(count, SIDE, SIDE)


def finish(done, last, wide, out_hbm, sheets, sem):
    ready = done.shape[0]
    pltpu.make_async_copy(done, out_hbm.at[pl.ds(0, ready)], sem).start()
    for first in range(0, last.shape[0], 2):
        sheets[first : first + 2] = last_product(last[first : first + 2], wide[...])
        pltpu.make_async_copy(
            sheets.at[pl.ds(first, 2)], out_hbm.at[pl.ds(ready + first, 2)], sem
        ).start()
    pltpu.make_async_copy(out_hbm, out_hbm, sem).wait()


def shards(side, orbitals, point_index):
    orbital_count, cells = orbitals.shape
    chips = side * side
    points = point_index.shape[0] // (2 * chips)
    others = chips - 1
    part_points = points // 2
    dma = pltpu.SemaphoreType.DMA
    in_place = functools.partial(pltpu.with_memory_space_constraint, memory_space=pltpu.HBM)
    groups = 1 + len(REST_GROUPS)
    done, last, wide = pl.pallas_call(
        functools.partial(body, side, points),
        out_shape=[
            jax.ShapeDtypeStruct((part_points, SIDE, SIDE), F32),
            jax.ShapeDtypeStruct((part_points, SIDE, 2 * SIDE), BF16),
            jax.ShapeDtypeStruct((2 * SIDE, 2 * SIDE), BF16),
        ],
        in_specs=[pl.BlockSpec(memory_space=pltpu.HBM)] * 2,
        out_specs=[pl.BlockSpec(memory_space=pltpu.VMEM)] * 3,
        scratch_shapes=[
            pltpu.VMEM((2, orbital_count, cells), BF16),
            pltpu.VMEM((1, point_index.shape[0]), jnp.int32),
            pltpu.VMEM((chips * points, cells), BF16),
            pltpu.VMEM((2, side, side, part_points, orbital_count), BF16),
            pltpu.VMEM((2, side, side, part_points, orbital_count), BF16),
            pltpu.VMEM((side, 2, side, part_points, orbital_count), BF16),
            pltpu.VMEM((side, 2, side, part_points, orbital_count), BF16),
            pltpu.VMEM((2, side - 1, side, part_points, orbital_count), BF16),
            pltpu.VMEM((2, side, part_points, orbital_count), BF16),
            pltpu.VMEM((2, side - 1, side, part_points, orbital_count), BF16),
            pltpu.VMEM((2, side, side, part_points, orbital_count), BF16),
            pltpu.VMEM((2, side, side, part_points, 2 * cells), jnp.int16),
            pltpu.VMEM((2, side, side, 1, SIDE), F32),
            pltpu.VMEM((2, others, part_points, 2 * cells), jnp.int16),
            pltpu.VMEM((2, others, 1, SIDE), F32),
            pltpu.VMEM((2, SIDE * part_points, SIDE), F32),
            pltpu.VMEM((2 * SIDE, 2 * SIDE), BF16),
            pltpu.VMEM((SIDE, SIDE), F32),
            pltpu.VMEM((2, part_points // 2, 2 * SIDE, 2 * SIDE), BF16),
            pltpu.VMEM((part_points, SIDE, 2 * SIDE), BF16),
            dma((2,)), dma, dma((side,)), dma, dma,
            dma((3,)), dma((2,)), dma((2,)), dma((2,)),
            dma, dma((2, groups)), dma, dma((2, groups)),
        ],
        compiler_params=pltpu.CompilerParams(
            collective_id=0, has_side_effects=True, vmem_limit_bytes=VMEM_BYTES
        ),
    )(in_place(orbitals), in_place(point_index.reshape(1, -1)))
    out = pl.pallas_call(
        finish,
        out_shape=jax.ShapeDtypeStruct((points, SIDE, SIDE), F32),
        in_specs=[pl.BlockSpec(memory_space=pltpu.VMEM)] * 3,
        out_specs=pl.BlockSpec(memory_space=pltpu.HBM),
        scratch_shapes=[pltpu.VMEM((part_points, SIDE, SIDE), F32), dma],
        compiler_params=pltpu.CompilerParams(vmem_limit_bytes=8 * 1024 * 1024),
    )(done, last, wide)
    return out[None]


def solution(mesh):
    grid_count = mesh.shape["grid"]
    size = math.isqrt(grid_count // 2)
    in_specs = (P(None, "grid"), P("pts"))
    out_specs = P("pts", "grid", None, None)
    step = functools.partial(shards, size)
    return jax.shard_map(step, mesh=mesh, in_specs=in_specs, out_specs=out_specs, check_vma=False)
```

```python
import functools
import math

import jax
import jax.numpy as jnp
from jax import lax
from jax.experimental import pallas as pl
from jax.experimental.pallas import tpu as pltpu
from jax.sharding import PartitionSpec as P

SIDE = 128
MESH = pl.DeviceIdType.MESH
F32 = jnp.float32
BF16 = jnp.bfloat16
TOP = 32766.0
FLOOR = 1e-30
REST_GROUPS = (12,)
VMEM_BYTES = 16 * 1024 * 1024


def split(values):
    high = values.astype(BF16)
    return high, (values - high.astype(F32)).astype(BF16)


def cas_table():
    rows = lax.broadcasted_iota(jnp.int32, (SIDE, SIDE), 0)
    columns = lax.broadcasted_iota(jnp.int32, (SIDE, SIDE), 1)
    angles = ((rows * columns) % SIDE).astype(F32) * (2.0 * math.pi / SIDE)
    return jnp.cos(angles) + jnp.sin(angles)


def screen_kernel():
    rows = lax.broadcasted_iota(jnp.int32, (SIDE, SIDE), 0)
    columns = lax.broadcasted_iota(jnp.int32, (SIDE, SIDE), 1)
    across = jnp.minimum(rows, SIDE - rows).astype(F32)
    along = jnp.minimum(columns, SIDE - columns).astype(F32)
    screening = SIDE / 16.0
    values = screening / jnp.sqrt(across * across + along * along + screening * screening)
    return jnp.where((rows == 0) & (columns == 0), 0.0, values * (1.0 / (SIDE * SIDE)))


def offsets(size_y, size_x):
    far = lambda d, n: min(d, n - d)
    every = [(dy, dx) for dy in range(size_y) for dx in range(size_x) if (dy, dx) != (0, 0)]
    return sorted(every, key=lambda o: (-far(o[0], size_y) - far(o[1], size_x), o))


def body(
    side, points,
    orb_hbm, idx_hbm, done, last, wide,
    phi, idx, their_mask, mine, theirs, from_sib, part, first_in, summed, second_in, vectors, quant, scale, quant_in, scale_in,
    rows_done, tall, kern, middle, first_last,
    load_sem, sib_send, sib_recv, orb_send, orb_recv, p_send, first_recv, second_recv, third_recv,
    q_send, q_recv, s_send, s_recv,
):
    me = lax.axis_index("grid")
    core = me % 2
    chip = me // 2
    my_y = chip // side
    my_x = chip % side
    chips = side * side
    cells = phi.shape[2]
    orbital_count = phi.shape[1]
    part_points = points // 2
    offs = offsets(side, side)
    count = len(offs)
    steps = [2, 1, 3][-(side - 1) :]
    flavours = range(2)
    first_at = (my_x, my_y)
    second_at = (my_y, my_x)

    def at(dy, dx):
        return ((my_y + dy + side) % side) * side + (my_x + dx + side) % side

    def device(c):
        return {"grid": c * 2 + core}

    def along_first(f, e):
        return device(at(0, e) if f == 0 else at(e, 0))

    def along_second(f, e):
        return device(at(e, 0) if f == 0 else at(0, e))

    def remote(src, dst, send, recv, to):
        return pltpu.make_async_remote_copy(
            src_ref=src, dst_ref=dst, send_sem=send, recv_sem=recv, device_id=to, device_id_type=MESH
        )

    def wait_all(ref, sem):
        pltpu.make_async_copy(ref, ref, sem).wait()

    sibling = {"grid": chip * 2 + 1 - core}

    with jax.named_scope("signals"):
        load_idx = pltpu.make_async_copy(idx_hbm, idx, load_sem.at[1])
        load_idx.start()
        load_orb = pltpu.make_async_copy(orb_hbm, phi.at[core], load_sem.at[0])
        load_orb.start()
        barrier = pltpu.get_barrier_semaphore()
        pl.semaphore_signal(barrier, inc=1, device_id=sibling, device_id_type=MESH)
        for e in steps:
            for f in flavours:
                pl.semaphore_signal(barrier, inc=1, device_id=along_first(f, e), device_id_type=MESH)

    with jax.named_scope("indices"):
        load_idx.wait()
        total = idx.shape[1]
        column = jnp.transpose(jnp.broadcast_to(idx[...], (SIDE, total))) - me * cells
        column = column.reshape(chips, 2, points, SIDE)
        lane = lax.broadcasted_iota(jnp.int32, (chips * points, SIDE), 1)

    def mask_of(layer):
        chosen = jnp.where(layer == 0, column[:, 0], column[:, 1]).reshape(chips * points, SIDE)
        return jnp.concatenate(
            [jnp.where(chosen == lane + j * SIDE, 1.0, 0.0).astype(BF16) for j in range(cells // SIDE)], axis=1
        )

    def owned(mask, to):
        found = lax.dot_general(mask, phi[core], (((1,), (1,)), ((), ())), preferred_element_type=F32)
        for y in range(side):
            for x in range(side):
                at_row = (y * side + x) * points
                to[0, x, y] = found[at_row : at_row + part_points].astype(BF16)
                to[1, y, x] = found[at_row + part_points : at_row + points].astype(BF16)

    with jax.named_scope("ownpicks"):
        their_mask[...] = mask_of(1 - core)
        load_orb.wait()
        owned(their_mask[...], theirs)

    with jax.named_scope("barrier"):
        pl.semaphore_wait(barrier, 2 * len(steps) + 1)

    with jax.named_scope("sibstart"):
        for n, e in enumerate(steps + [0]):
            for f in flavours:
                line = (first_at[f] + e) % side
                remote(theirs.at[f, line], from_sib.at[n, f], sib_send, sib_recv.at[n], sibling).start()
    with jax.named_scope("minepicks"):
        owned(mask_of(core), mine)

    for n, e in enumerate(steps + [0]):
        with jax.named_scope("sibling%d" % n):
            wait_all(from_sib.at[n], sib_recv.at[n])
        with jax.named_scope("first%d" % n):
            for f in flavours:
                line = (first_at[f] + e) % side
                part[n, f] = mine[f, line] + from_sib[n, f]
                if e:
                    remote(
                        part.at[n, f], first_in.at[f, n], p_send.at[0], first_recv.at[f], along_first(f, e)
                    ).start()

    to_sibling = remote(phi.at[core], phi.at[core], orb_send, orb_recv, sibling)
    to_sibling.start()

    with jax.named_scope("tables"):
        high, low = split(cas_table())
        wide[0:SIDE, 0:SIDE] = high
        wide[0:SIDE, SIDE:] = low
        wide[SIDE:, 0:SIDE] = high
        wide[SIDE:, SIDE:] = low
        tall[0:SIDE, 0:SIDE] = high
        tall[0:SIDE, SIDE:] = high
        tall[SIDE:, 0:SIDE] = low
        tall[SIDE:, SIDE:] = low
        kern[...] = screen_kernel()

    def homes(h):
        return pl.ds(h * (side // 2), side // 2)

    halves = range(2)
    own_line = len(steps)
    for f in flavours:
        with jax.named_scope("firstwait%d" % f):
            wait_all(first_in.at[f], first_recv.at[f])
        with jax.named_scope("second%d" % f):
            for h in halves:
                value = part[own_line, f, homes(h)]
                for n in range(len(steps)):
                    value = value + first_in[f, n, homes(h)]
                summed[f, h] = value
                for n, e in enumerate(steps):
                    remote(
                        summed.at[f, h], second_in.at[f, h, n], p_send.at[1], second_recv.at[f, h],
                        along_second(f, e),
                    ).start()
    for h in halves:
        for f in flavours:
            with jax.named_scope("secondwait%d%d" % (h, f)):
                wait_all(second_in.at[f, h], second_recv.at[f, h])
            with jax.named_scope("third%d%d" % (h, f)):
                value = summed[f, h]
                for n in range(len(steps)):
                    value = value + second_in[f, h, n]
                line = first_at[f]
                vectors[f, line, homes(h)] = value
                for e in steps:
                    here = vectors.at[f, line, homes(h)]
                    remote(here, here, p_send.at[2], third_recv.at[f], along_first(f, e)).start()

    slots = [
        [o for o in offs if o[1 - f] == 0] + [o for o in offs if o[1 - f] != 0] for f in flavours
    ]
    sizes = (len(steps),) + REST_GROUPS
    bounds = [sum(sizes[:g]) for g in range(len(sizes) + 1)]

    def back_copies(f, g):
        copies = []
        for n in range(bounds[g], bounds[g + 1]):
            dy, dx = slots[f][n]
            line, place = ((dx, (my_y + dy) % side), (dy, (my_x + dx) % side))[f]
            to = device(at(dy, dx))
            copies.append(remote(scale.at[f, line, place], scale_in.at[f, n], s_send, s_recv.at[f, g], to))
            copies.append(remote(quant.at[f, line, place], quant_in.at[f, n], q_send, q_recv.at[f, g], to))
        return copies

    diagonal = lax.broadcasted_iota(jnp.int32, (part_points, SIDE), 0) == lax.broadcasted_iota(
        jnp.int32, (part_points, SIDE), 1
    )

    def pairs(f, lines):
        size = len(lines) * side * part_points
        block = jnp.concatenate(
            [vectors[f, (first_at[f] + r) % side].reshape(side * part_points, orbital_count) for r in lines], axis=0
        )
        pair = jnp.concatenate([jnp.dot(block, phi[h], preferred_element_type=F32) for h in range(2)], axis=1)
        peak = jnp.maximum(jnp.max(jnp.abs(pair), axis=1, keepdims=True), FLOOR)
        coded = jnp.round(pair * (TOP / peak)).astype(jnp.int32)
        step = jnp.broadcast_to(peak * (1.0 / TOP), (size, SIDE))
        for n, r in enumerate(lines):
            for place in range(side):
                rows = slice((n * side + place) * part_points, (n * side + place + 1) * part_points)
                quant[f, r, place] = coded[rows].astype(jnp.int16)
                scale[f, r, place] = jnp.sum(jnp.where(diagonal, step[rows], 0.0), axis=0, keepdims=True)

    to_sibling.wait()
    for f in flavours:
        with jax.named_scope("early%d" % f):
            pairs(f, [0])
            for copy in back_copies(f, 0):
                copy.start()
    for f in flavours:
        with jax.named_scope("gather%d" % f):
            wait_all(first_in.at[f], third_recv.at[f])
        with jax.named_scope("pairs%d" % f):
            pairs(f, steps)
            for g in range(1, len(sizes)):
                for copy in back_copies(f, g):
                    copy.start()

    rows = 2 * cells // SIDE

    def along(f, blocks):
        stacks = []
        for block, row_of, _ in blocks:
            step = jnp.sum(
                jnp.where(diagonal, jnp.broadcast_to(row_of, (part_points, SIDE)), 0.0), axis=1, keepdims=True
            )
            pair = block.astype(jnp.int32).astype(F32) * step
            square = pair * pair
            stacks.extend(square[:, r * SIDE : (r + 1) * SIDE] for r in range(rows))
        high, low = split(jnp.concatenate(stacks, axis=0))
        product = jnp.dot(jnp.concatenate([high, low], axis=1), wide[...], preferred_element_type=F32)
        product = product[:, :SIDE] + product[:, SIDE:]
        size = rows * part_points
        for n, (_, _, source) in enumerate(blocks):
            rows_done[f, pl.ds(pl.multiple_of(source * size, size), size), :] = product[n * size : (n + 1) * size]

    def across(f):
        weight = jnp.concatenate([kern[...], kern[...]], axis=1)
        for n in range(part_points // 2):
            pieces = [rows_done[f, pl.ds(p, SIDE, stride=part_points), :] for p in (2 * n, 2 * n + 1)]
            high, low = split(jnp.concatenate(pieces, axis=1))
            product = jnp.dot(tall[...], jnp.concatenate([high, low], axis=0), preferred_element_type=F32)
            high, low = split((product[:SIDE] + product[SIDE:]) * weight)
            middle[f, n, 0:SIDE] = high
            middle[f, n, SIDE:] = low
        for n in range(part_points // 2):
            product = jnp.dot(tall[...], middle[f, n], preferred_element_type=F32)
            high, low = split(product[:SIDE] + product[SIDE:])
            for p in range(2):
                lanes = slice(p * SIDE, (p + 1) * SIDE)
                to = (first_last, last)[f]
                to[2 * n + p, :, 0:SIDE] = high[:, lanes]
                to[2 * n + p, :, SIDE:] = low[:, lanes]

    for f, g in [(0, 0), (1, 0)] + [(f, g) for f in flavours for g in range(1, len(sizes))]:
        group = range(bounds[g], bounds[g + 1])
        with jax.named_scope("wait%d%d" % (f, g)):
            wait_all(quant_in.at[f, pl.ds(bounds[g], sizes[g])], q_recv.at[f, g])
            wait_all(scale_in.at[f, pl.ds(bounds[g], sizes[g])], s_recv.at[f, g])
        with jax.named_scope("along%d%d" % (f, g)):
            blocks = [
                (quant_in[f, n], scale_in[f, n], at(-slots[f][n][0], -slots[f][n][1])) for n in group
            ]
            if g == 0:
                blocks.append((quant[f, 0, second_at[f]], scale[f, 0, second_at[f]], chip))
            along(f, blocks)
        if g == len(sizes) - 1:
            with jax.named_scope("across%d" % f):
                across(f)
            if f == 0:
                with jax.named_scope("output"):
                    for first in range(0, part_points, 2):
                        done[first : first + 2] = last_product(first_last[first : first + 2], wide[...])

    with jax.named_scope("sends"):
        wait_all(from_sib, sib_send)
        for n in range(3):
            wait_all(first_in, p_send.at[n])
        wait_all(quant_in, q_send)
        wait_all(scale_in, s_send)


def last_product(values, wide):
    count = values.shape[0]
    product = jnp.dot(values.reshape(count * SIDE, 2 * SIDE), wide, preferred_element_type=F32)
    return (product[:, :SIDE] + product[:, SIDE:]).reshape(count, SIDE, SIDE)


def finish(done, last, wide, out_hbm, sheets, sem):
    ready = done.shape[0]
    pltpu.make_async_copy(done, out_hbm.at[pl.ds(0, ready)], sem).start()
    for first in range(0, last.shape[0], 2):
        sheets[first : first + 2] = last_product(last[first : first + 2], wide[...])
        pltpu.make_async_copy(
            sheets.at[pl.ds(first, 2)], out_hbm.at[pl.ds(ready + first, 2)], sem
        ).start()
    pltpu.make_async_copy(out_hbm, out_hbm, sem).wait()


def shards(side, orbitals, point_index):
    orbital_count, cells = orbitals.shape
    chips = side * side
    points = point_index.shape[0] // (2 * chips)
    others = chips - 1
    part_points = points // 2
    dma = pltpu.SemaphoreType.DMA
    in_place = functools.partial(pltpu.with_memory_space_constraint, memory_space=pltpu.HBM)
    groups = 1 + len(REST_GROUPS)
    done, last, wide = pl.pallas_call(
        functools.partial(body, side, points),
        out_shape=[
            jax.ShapeDtypeStruct((part_points, SIDE, SIDE), F32),
            jax.ShapeDtypeStruct((part_points, SIDE, 2 * SIDE), BF16),
            jax.ShapeDtypeStruct((2 * SIDE, 2 * SIDE), BF16),
        ],
        in_specs=[pl.BlockSpec(memory_space=pltpu.HBM)] * 2,
        out_specs=[pl.BlockSpec(memory_space=pltpu.VMEM)] * 3,
        scratch_shapes=[
            pltpu.VMEM((2, orbital_count, cells), BF16),
            pltpu.VMEM((1, point_index.shape[0]), jnp.int32),
            pltpu.VMEM((chips * points, cells), BF16),
            pltpu.VMEM((2, side, side, part_points, orbital_count), BF16),
            pltpu.VMEM((2, side, side, part_points, orbital_count), BF16),
            pltpu.VMEM((side, 2, side, part_points, orbital_count), BF16),
            pltpu.VMEM((side, 2, side, part_points, orbital_count), BF16),
            pltpu.VMEM((2, side - 1, side, part_points, orbital_count), BF16),
            pltpu.VMEM((2, 2, side // 2, part_points, orbital_count), BF16),
            pltpu.VMEM((2, 2, side - 1, side // 2, part_points, orbital_count), BF16),
            pltpu.VMEM((2, side, side, part_points, orbital_count), BF16),
            pltpu.VMEM((2, side, side, part_points, 2 * cells), jnp.int16),
            pltpu.VMEM((2, side, side, 1, SIDE), F32),
            pltpu.VMEM((2, others, part_points, 2 * cells), jnp.int16),
            pltpu.VMEM((2, others, 1, SIDE), F32),
            pltpu.VMEM((2, SIDE * part_points, SIDE), F32),
            pltpu.VMEM((2 * SIDE, 2 * SIDE), BF16),
            pltpu.VMEM((SIDE, SIDE), F32),
            pltpu.VMEM((2, part_points // 2, 2 * SIDE, 2 * SIDE), BF16),
            pltpu.VMEM((part_points, SIDE, 2 * SIDE), BF16),
            dma((2,)), dma, dma((side,)), dma, dma,
            dma((3,)), dma((2,)), dma((2, 2)), dma((2,)),
            dma, dma((2, groups)), dma, dma((2, groups)),
        ],
        compiler_params=pltpu.CompilerParams(
            collective_id=0, has_side_effects=True, vmem_limit_bytes=VMEM_BYTES
        ),
    )(in_place(orbitals), in_place(point_index.reshape(1, -1)))
    out = pl.pallas_call(
        finish,
        out_shape=jax.ShapeDtypeStruct((points, SIDE, SIDE), F32),
        in_specs=[pl.BlockSpec(memory_space=pltpu.VMEM)] * 3,
        out_specs=pl.BlockSpec(memory_space=pltpu.HBM),
        scratch_shapes=[pltpu.VMEM((part_points, SIDE, SIDE), F32), dma],
        compiler_params=pltpu.CompilerParams(vmem_limit_bytes=8 * 1024 * 1024),
    )(done, last, wide)
    return out[None]


def solution(mesh):
    grid_count = mesh.shape["grid"]
    size = math.isqrt(grid_count // 2)
    in_specs = (P(None, "grid"), P("pts"))
    out_specs = P("pts", "grid", None, None)
    step = functools.partial(shards, size)
    return jax.shard_map(step, mesh=mesh, in_specs=in_specs, out_specs=out_specs, check_vma=False)
```
